256 devices in a mesh: sta: 32 (over z, x), sat: 8 (over y, core).
Axes of the slice: x: 4, y: 4, z: 8, core: 2. Of those that a mesh axis runs over, the one named last changes fastest.
Arguments:
- sight: float32 [512, 3, 32, 256], P(('sta', 'sat')), may hold values from -1 to 1
- mapping: float32 [512, 32, 256], P(('sta', 'sat')), may hold values from 1 to 10
- residual: float32 [512, 32, 256], P(('sta', 'sat')), may hold values from -6 to 6
- counts: int32 [512, 32, 256], P(('sta', 'sat')), may hold values from 0 to 3, as said below
- track: int32 [512, 32], P(('sta', 'sat')), may hold values from 0 to 119, all different within a row
- knots: int32 [512, 256], P(('sta', 'sat')), may hold values from 0 to 3, as said below
- orbit: float32 [120, 3, 8, 256], P('sat'), may hold values from -6 to 6
Outputs:
- normal: float32 [960, 960], P('sat', 'sta')
- right_hand: float32 [960], P('sat')
- own_blocks: float32 [120, 8, 8], P('sat')
The draws below stay inside these ranges and needn't reach their ends.
Inputs may be any that keep to these rules, and one draw needn't show every extreme that they name: `track`: each station's row names 32 different satellites, and every satellite is tracked by some station. `knots`: along the epochs of each station the index never falls, and every index from 0 to 3 occurs for every station. `counts`: some stations observe no satellite at all over a run of epochs.
All inputs are finite; a program needn't handle non-finite values.
Results may differ from the reference program's by a relative error of at most 0.00012.
Values sent between devices are 32-bit elements; how exact they have to be, the bound alone decides.
A program may use at most 256 MiB of HBM per device.

```python
import math
import jax
import jax.numpy as jnp
from jax import lax

SATS = 120
PAR = 8
TRACK = 32
EPOCHS = 256
KNOTS = 4
STATIONS = 512


def draw_knots(key, part):
    span = EPOCHS // KNOTS
    offsets = jax.random.randint(jax.random.fold_in(key, 7), (STATIONS, 1), 0, span)
    epoch_steps = jnp.arange(EPOCHS, dtype=jnp.int32)[None, :]
    return jnp.minimum((epoch_steps + offsets) // span, KNOTS - 1).astype(jnp.int32)


def draw_counts(key, part):
    longest = max(1, EPOCHS // 8)
    base = jax.random.randint(jax.random.fold_in(key, 11), (STATIONS, TRACK, EPOCHS), 0, 4)
    offset = jax.random.randint(jax.random.fold_in(key, 12), (), 0, 32)
    station_ids = jnp.arange(STATIONS, dtype=jnp.int32)
    outage_station = (station_ids + offset) % 32 == 0
    first_dead = jax.random.randint(jax.random.fold_in(key, 13), (STATIONS, 1), 0, EPOCHS - longest + 1)
    dead_length = jax.random.randint(jax.random.fold_in(key, 14), (STATIONS, 1), 1, longest + 1)
    epoch_steps = jnp.arange(EPOCHS, dtype=jnp.int32)[None, :]
    dead = outage_station[:, None] & (epoch_steps >= first_dead) & (epoch_steps < first_dead + dead_length)
    return jnp.where(dead[:, None, :], 0, base).astype(jnp.int32)


def block_scale(own_key, shape, pieces, least, top_value):
    level = 1.0
    for dim, parts in pieces:
        draws = jax.random.uniform(jax.random.fold_in(jax.random.fold_in(own_key, 6), dim), (parts,), jnp.float32, least / len(pieces), top_value / len(pieces))
        level = level * jnp.repeat(jnp.exp(draws), shape[dim] // parts).reshape((-1,) + (1,) * (len(shape) - 1 - dim))
    return level


def picks_of(stream_key, rows, amount, top, lift):
    ranking = jax.random.permutation(jax.random.fold_in(stream_key, 1), amount)
    pull = ranking
    for power in range(3):
        pull = pull * pull // amount
    pull = pull * lift // amount
    chance = jax.random.randint(jax.random.fold_in(stream_key, 2), (rows, amount), 0, 4096) + pull
    sure = jax.random.permutation(jax.random.fold_in(stream_key, 3), rows)[jnp.arange(amount) % rows]
    chance = jnp.where(jnp.arange(rows)[:, None] == sure[None, :], 1 << 14, chance)
    priority = chance * amount + jnp.arange(amount)
    return lax.top_k(priority.astype(jnp.int32), top)[1].astype(jnp.int32)


def scatter_about(stream_key, extent, width, most, split=(), kind=jnp.bfloat16):
    result = jax.random.normal(stream_key, extent, jnp.float32) * width
    if len(split) > 0:
        result = block_scale(stream_key, extent, split, -0.22, 0.18) * result
    return jnp.clip(result, min=-most, max=most).astype(kind)


def setup_inputs(seed: int = 0) -> dict:
    streams_of = jax.random.split(jax.random.key(seed), 8)
    return {
        "sight": jnp.clip(jax.random.uniform(streams_of[0], (STATIONS, 3, TRACK, EPOCHS), jnp.float32, -1.0, 1.0) * block_scale(streams_of[0], (STATIONS, 3, TRACK, EPOCHS), ((0, 256),), -0.4, 0.0), -1.0, 1.0),
        "mapping": jnp.clip(jnp.exp(math.log(10.0) - 2.3025851 * jax.random.uniform(streams_of[1], (STATIONS, TRACK, EPOCHS), jnp.float32) ** block_scale(streams_of[1], (STATIONS, TRACK, EPOCHS), ((0, 256),), -0.2, 0.2)), 1.0, 10.0),
        "residual": scatter_about(streams_of[2], (STATIONS, TRACK, EPOCHS), 1.0, 6.0, ((0, 256),), jnp.float32),
        "counts": draw_counts(jax.random.fold_in(streams_of[7], 71), 0),
        "track": picks_of(streams_of[4], STATIONS, SATS, TRACK, 2184),
        "knots": draw_knots(jax.random.fold_in(streams_of[7], 71), 0),
        "orbit": scatter_about(streams_of[6], (SATS, 3, PAR, EPOCHS), 1.0, 6.0, ((0, 8),), jnp.float32),
    }


PRIOR = 1.0
HIGH = lax.Precision.HIGHEST

def reduce_station(station_sight, station_map, station_res, station_count, station_track, station_knot, orbit):
    tracked = station_sight.shape[1]
    epochs = station_sight.shape[2]
    params = orbit.shape[2]
    span = tracked * params
    tracked_orbit = jnp.take(orbit, station_track, axis=0)
    design = lax.optimization_barrier(jnp.sum(jnp.transpose(station_sight, (1, 0, 2))[:, :, None, :] * tracked_orbit, axis=1))
    weight = station_count.astype(jnp.float32)
    epoch_total = jnp.maximum(lax.optimization_barrier(jnp.sum(weight, 0)), 1.0)
    weighted = design * weight[:, None, :]
    weighted_rows = weighted.reshape(span, epochs)
    design_rows = design.reshape(span, epochs)
    clock_term = jnp.dot(weighted_rows / epoch_total, weighted_rows.T, precision=HIGH)
    slot_of = jnp.arange(span, dtype=jnp.int32) // params
    block_mask = (slot_of[:, None] == slot_of[None, :]).astype(jnp.float32)
    station_normal = jnp.dot(weighted_rows, design_rows.T, precision=HIGH) * block_mask - clock_term
    knot_select = (station_knot[None, :] == jnp.arange(KNOTS, dtype=jnp.int32)[:, None]).astype(jnp.float32)
    weight_map = weight * station_map
    sum_map = lax.optimization_barrier(jnp.sum(weight_map, 0))
    sum_res = lax.optimization_barrier(jnp.sum(weight * station_res, 0))
    tropo_rows = (weighted * station_map[:, None, :]).reshape(span, epochs) - weighted_rows * (sum_map / epoch_total)
    tropo_cross = jnp.dot(tropo_rows, knot_select.T, precision=HIGH)
    tropo_diag = jnp.dot(knot_select, lax.optimization_barrier(jnp.sum(weight_map * station_map, 0)) - sum_map * sum_map / epoch_total, precision=HIGH) + PRIOR
    right_global = lax.optimization_barrier(jnp.sum((weighted * station_res[:, None, :]).reshape(span, epochs) - weighted_rows * (sum_res / epoch_total), 1))
    right_local = jnp.dot(knot_select, lax.optimization_barrier(jnp.sum(weight_map * station_res, 0)) - sum_map * sum_res / epoch_total, precision=HIGH)
    scaled_cross = tropo_cross / tropo_diag
    station_normal = station_normal - jnp.dot(scaled_cross, tropo_cross.T, precision=HIGH)
    station_right = right_global - jnp.dot(scaled_cross, right_local, precision=HIGH)
    global_columns = (station_track[:, None] * params + jnp.arange(params, dtype=jnp.int32)[None, :]).reshape(span).astype(jnp.int32)
    return (station_normal, station_right, global_columns)

def reference(sight, mapping, residual, counts, track, knots, orbit):
    full_width = SATS * PAR

    def visit(station, carry):
        normal_sum, right_sum = carry
        station_normal, station_right, global_columns = reduce_station(sight[station], mapping[station], residual[station], counts[station], track[station], knots[station], orbit)
        normal_sum = normal_sum.at[global_columns[:, None], global_columns[None, :]].add(station_normal)
        right_sum = right_sum.at[global_columns].add(station_right)
        return (normal_sum, right_sum)
    start = (jnp.zeros((full_width, full_width), jnp.float32), jnp.zeros((full_width,), jnp.float32))
    normal_sum, right_sum = lax.fori_loop(0, STATIONS, visit, start)
    factor = SATS / (STATIONS * TRACK * EPOCHS)
    cross_factor = SATS / math.sqrt(STATIONS * EPOCHS)
    tiled = normal_sum.reshape(SATS, PAR, SATS, PAR)
    own_blocks = jnp.transpose(jnp.diagonal(tiled, axis1=0, axis2=2), (2, 0, 1)) * factor
    owner_of = jnp.arange(full_width, dtype=jnp.int32) // PAR
    cross_part = jnp.where(owner_of[:, None] == owner_of[None, :], 0.0, normal_sum) * cross_factor
    return (cross_part, right_sum * factor, own_blocks)
```

```python
import functools
import math

import jax
import jax.numpy as jnp
from jax import lax
from jax.experimental import pallas as pl
from jax.experimental.pallas import tpu as pltpu
from jax.sharding import PartitionSpec as P

F32 = jnp.float32
BF16 = jnp.bfloat16
MESH = pl.DeviceIdType.MESH
HIGH = lax.Precision.HIGHEST

SATS = 120
OWN = 15
PAR = 8
SLOTS = 32
EPOCHS = 256
KNOTS = 4
PRIOR = 1.0
NY = 4
NX = 4
NZ = 8
ROWS = 120
COVER = 40
CUT = 8
ZA = 5
ANY = pl.BlockSpec(memory_space=pl.ANY)
VMEM = pl.BlockSpec(memory_space=pltpu.VMEM)
SMEM = pl.BlockSpec(memory_space=pltpu.SMEM)


def place():
    sta = lax.axis_index("sta")
    sat = lax.axis_index("sat")
    return sta // NX, sta % NX, sat // 2, sat % 2


def remote(src, dst, send, recv, device):
    return pltpu.make_async_remote_copy(
        src_ref=src,
        dst_ref=dst,
        send_sem=send,
        recv_sem=recv,
        device_id=device,
        device_id_type=MESH,
    )


def greet(peers):
    barrier = pltpu.get_barrier_semaphore()
    for peer in peers:
        pl.semaphore_signal(barrier, inc=1, device_id=peer, device_id_type=MESH)
    pl.semaphore_wait(barrier, len(peers))


def gather_kernel(*refs):
    orbit = refs[0]
    stations = refs[1:7]
    full = refs[7]
    others = refs[8:14]
    send, recv, local = refs[14:]
    z, x, y, c = place()
    sta = z * NX + x
    right = (sta, ((y + 1) % NY) * 2 + c)
    left = (sta, ((y + NY - 1) % NY) * 2 + c)
    mate = (sta, y * 2 + 1 - c)
    greet((right, left, mate))

    mine = (y * 2 + c) * OWN
    from_left = (((y + NY - 1) % NY) * 2 + c) * OWN
    from_right = (((y + 1) % NY) * 2 + c) * OWN
    from_far = (((y + 2) % NY) * 2 + c) * OWN
    head, tail = (0, CUT), (CUT, OWN - CUT)

    def part(base, cut):
        return full.at[pl.ds(base + cut[0], cut[1])]

    def own(cut):
        return orbit.at[pl.ds(cut[0], cut[1])]

    def go(slot, src, dst, device):
        copy = remote(src, dst, send.at[slot], recv.at[slot], device)
        copy.start()
        return copy

    copies = []
    right_head = go(0, own(head), part(mine, head), right)
    left_tail = go(1, own(tail), part(mine, tail), left)
    right_tail = go(2, own(tail), part(mine, tail), right)
    left_head = go(3, own(head), part(mine, head), left)
    keep = pltpu.make_async_copy(orbit, full.at[pl.ds(mine, OWN)], local)
    keep.start()
    mates = [go(6 + i, a, b, mate) for i, (a, b) in enumerate(zip(stations, others))]
    mates.append(go(12, orbit, full.at[pl.ds(mine, OWN)], mate))

    right_head.wait_recv()
    relay_right = go(4, part(from_left, head), part(from_left, head), right)
    mates.append(go(13, part(from_left, head), part(from_left, head), mate))
    left_tail.wait_recv()
    relay_left = go(5, part(from_right, tail), part(from_right, tail), left)
    mates.append(go(14, part(from_right, tail), part(from_right, tail), mate))
    right_tail.wait_recv()
    mates.append(go(15, part(from_left, tail), part(from_left, tail), mate))
    left_head.wait_recv()
    mates.append(go(16, part(from_right, head), part(from_right, head), mate))
    relay_right.wait_recv()
    mates.append(go(17, part(from_far, head), part(from_far, head), mate))
    relay_left.wait_recv()
    mates.append(go(18, part(from_far, tail), part(from_far, tail), mate))
    for copy in mates:
        copy.wait_recv()
    for copy in (right_head, left_tail, right_tail, left_head, relay_right, relay_left):
        copy.wait_send()
    for copy in mates:
        copy.wait_send()
    keep.wait()


def halves(value):
    high = value.astype(BF16)
    low = (value - high.astype(F32)).astype(BF16)
    return high, low


def turned(a, b, precision=None):
    return lax.dot_general(
        a, b, (((1,), (1,)), ((), ())), preferred_element_type=F32, precision=precision
    )


def product(a_high, a_low, b_high, b_low):
    return turned(a_high, b_high) + turned(a_high, b_low) + turned(a_low, b_high)


def tile_of(sat):
    group = sat // OWN
    return ((group % 2) * 4 + group // 2) * 16 + sat % OWN


def station_kernel(
    track_a, track_b, orbit, *refs
):
    mine = refs[0:5]
    other = refs[5:10]
    normal, small = refs[10:12]
    (factor, diagonal, extra, rows_w, rows_t, rows_r, rows_d, sides, f_high, f_low,
     r_high, r_low, e_high, e_low) = refs[12:]
    core = lax.axis_index("sat") % 2

    factor[...] = jnp.zeros_like(factor)
    diagonal[...] = jnp.zeros_like(diagonal)
    extra[...] = jnp.zeros_like(extra)
    local_rows = jnp.zeros((8, 128), F32)

    for index in range(4):
        sight, mapping, residual, counts, knots = mine if index < 2 else other
        track = track_a if index < 2 else track_b
        s = index % 2
        weight = counts[s].astype(F32)
        path = mapping[s]
        seen = residual[s]
        total = jnp.maximum(jnp.sum(weight, 0, keepdims=True), 1.0)
        share = 1.0 / total
        weight_map = weight * path
        sum_map = jnp.sum(weight_map, 0, keepdims=True)
        sum_res = jnp.sum(weight * seen, 0, keepdims=True)
        rows_w[...] = weight * lax.rsqrt(total)
        rows_t[...] = weight * (path - sum_map * share)
        rows_r[...] = weight * (seen - sum_res * share)
        rows_d[...] = jnp.sqrt(weight)
        square = jnp.sum(weight_map * path, 0, keepdims=True) - sum_map * sum_map * share
        cross = jnp.sum(weight_map * seen, 0, keepdims=True) - sum_map * sum_res * share
        lane_rows = lax.broadcasted_iota(jnp.int32, (128, EPOCHS), 0)
        pick = lane_rows == knots[s : s + 1, :] + KNOTS * index
        knot_rows = jnp.where(pick, 1.0, 0.0)
        last_rows = jnp.where(lane_rows == 16, 1.0, 0.0)
        row8 = lax.broadcasted_iota(jnp.int32, (8, EPOCHS), 0)
        pair = jnp.where(row8 == 0, square, jnp.where(row8 == 1, cross, 0.0))
        local_rows = local_rows + turned(pair, knot_rows, HIGH)
        lanes = slice(index * EPOCHS, (index + 1) * EPOCHS)

        def visit(m, carry):
            sat = track[s, m]
            tile = tile_of(sat)
            design = (
                sight[s, 0, pl.ds(m, 1), :] * orbit[sat, 0]
                + sight[s, 1, pl.ds(m, 1), :] * orbit[sat, 1]
                + sight[s, 2, pl.ds(m, 1), :] * orbit[sat, 2]
            )
            factor[tile, :, lanes] = design * rows_w[pl.ds(m, 1), :]
            diagonal[tile, :, lanes] = design * rows_d[pl.ds(m, 1), :]
            sides[m, :, 0:EPOCHS] = design * rows_t[pl.ds(m, 1), :]
            sides[m, :, EPOCHS : 2 * EPOCHS] = design * rows_r[pl.ds(m, 1), :]
            return carry

        lax.fori_loop(0, SLOTS, visit, 0, unroll=4)
        high, low = halves(sides[...].reshape(SLOTS * PAR, 2 * EPOCHS))
        pickers = jnp.concatenate([knot_rows, last_rows], axis=1).astype(BF16)
        crossed = (turned(high, pickers) + turned(low, pickers)).reshape(SLOTS, PAR, 128)
        sides[:, :, 0:128] = crossed

        def spread(m, carry):
            tile = tile_of(track[s, m])
            extra[tile] = extra[tile] + sides[m, :, 0:128]
            return carry

        lax.fori_loop(0, SLOTS, spread, 0, unroll=4)

    lane = lax.broadcasted_iota(jnp.int32, (1, 128), 1)
    scale = jnp.where(lane < 16, lax.rsqrt(local_rows[0:1] + PRIOR), 0.0)
    special = jnp.where(lane == 16, -1.0, local_rows[1:2] * scale)
    row = lax.broadcasted_iota(jnp.int32, (8, 128), 0)
    extra[15] = jnp.where(row == 0, special, 0.0)
    first = core * 64

    for block in range(8):
        rows = slice(block * 128, (block + 1) * 128)
        tiles = slice(block * 16, (block + 1) * 16)
        high, low = halves(factor[tiles].reshape(128, 4 * EPOCHS))
        f_high[rows, 0 : 4 * EPOCHS] = high
        f_low[rows, 0 : 4 * EPOCHS] = low
        side = extra[tiles].reshape(128, 128)
        if block == 0:
            special_row = lax.broadcasted_iota(jnp.int32, (128, 128), 0) >= ROWS
            side = jnp.where(special_row, side, side * scale)
        else:
            side = side * scale
        high, low = halves(side)
        f_high[rows, 4 * EPOCHS :] = high
        f_low[rows, 4 * EPOCHS :] = low

    tail = jnp.where(lane < 16, scale, 1.0)
    for block in range(4):
        rows = slice(block * 128, (block + 1) * 128)
        source = pl.ds(pl.multiple_of(core * 512, 512) + block * 128, 128)
        r_high[rows, 0 : 4 * EPOCHS] = f_high[source, 0 : 4 * EPOCHS]
        r_low[rows, 0 : 4 * EPOCHS] = f_low[source, 0 : 4 * EPOCHS]
        side = extra[pl.ds(first + block * 16, 16)].reshape(128, 128) * tail
        high, low = halves(side)
        r_high[rows, 4 * EPOCHS :] = high
        r_low[rows, 4 * EPOCHS :] = low

    for block in range(8):
        rows = slice(block * 128, (block + 1) * 128)
        result = product(f_high[rows], f_low[rows], r_high[...], r_low[...])
        group = (block % 4) * 2 + block // 4
        for slab in range(NY):
            normal[slab, group] = -result[:, slab * 128 : (slab + 1) * 128]

    own_row = lax.broadcasted_iota(jnp.int32, (128, 128), 0) // PAR
    own_lane = lax.broadcasted_iota(jnp.int32, (128, 128), 1) // PAR
    for slab in range(NY):
        high, low = halves(diagonal[pl.ds(first + slab * 16, 16)].reshape(128, 4 * EPOCHS))
        block = product(high, low, high, low) + normal[slab, slab * 2 + core]
        block = jnp.where(own_row == own_lane, block, 0.0).reshape(16, PAR, 128)
        small[slab, 0:8] = jnp.sum(block, 0)
        small[slab, 8:16] = normal[slab, 0, ROWS : ROWS + 8, :]


def ring_start(view, me, buffers, sems, device):
    far, right, left = (me + 2) % 4, (me + 1) % 4, (me + 3) % 4
    b_0, b_1, l_0, l_1, r_0, r_1 = buffers[:6]
    send, recv = sems
    plan = (
        (view(far, 0), b_0, right),
        (view(far, 1), b_1, left),
        (view(right, 1), l_1, right),
        (view(left, 0), r_0, left),
    )
    copies = []
    for slot, (src, dst, peer) in enumerate(plan):
        copy = remote(src, dst, send.at[slot], recv.at[slot], device(peer))
        copy.start()
        copies.append(copy)
    return copies


def ring_middle(view, me, buffers, sems, device, copies):
    right, left = (me + 1) % 4, (me + 3) % 4
    b_0, b_1, l_0, l_1, r_0, r_1, s_0, s_1 = buffers
    send, recv = sems
    copies[0].wait_recv()
    s_0[...] = view(right, 0)[...] + b_0[...]
    one = remote(s_0, l_0, send.at[4], recv.at[4], device(right))
    one.start()
    copies[1].wait_recv()
    s_1[...] = view(left, 1)[...] + b_1[...]
    two = remote(s_1, r_1, send.at[5], recv.at[5], device(left))
    two.start()
    return copies + [one, two]


def ring_finish(view, me, buffers, copies, out_0, out_1):
    b_0, b_1, l_0, l_1, r_0, r_1 = buffers[:6]
    for index in (2, 3, 4, 5):
        copies[index].wait_recv()
    out_0[...] = view(me, 0)[...] + l_0[...] + r_0[...]
    out_1[...] = view(me, 1)[...] + l_1[...] + r_1[...]


def reduce_kernel(normal, small, out, out_small, *refs):
    bufs = [refs[i * 8 : (i + 1) * 8] for i in range(4)]
    (y_part, x_part, total, arrived, small_y, small_x, small_z, hold_x, hold_z) = refs[32:41]
    sems = [(refs[41 + 2 * i], refs[42 + 2 * i]) for i in range(4)]
    z_send, z_recv, s_send, s_recv = refs[49:]
    z, x, y, c = place()

    def at_y(peer):
        return (z * NX + x, peer * 2 + c)

    def at_x(peer):
        return (z * NX + peer, y * 2 + c)

    def at_z(peer):
        return (peer * NX + x, y * 2 + c)

    greet(
        [at_y((y + k) % NY) for k in range(1, NY)]
        + [at_x((x + k) % NX) for k in range(1, NX)]
        + [at_z((z + k) % NZ) for k in range(1, NZ)]
    )

    def rows_of(peer):
        return pl.ds(pl.multiple_of(jnp.minimum(peer * 30 // 8, 10) * 8, 8), COVER)

    a_cut = (pl.ds(0, 3), pl.ds(3, ZA - 3))
    b_cut = (pl.ds(0, 2), pl.ds(2, 1))

    def ay_view(peer, half):
        return normal.at[peer, a_cut[half], pl.ds(0, ROWS)]

    def bx_view(peer, half):
        return normal.at[pl.ds(2 * half, 2), pl.ds(ZA, NZ - ZA), rows_of(peer)]

    def ax_view(peer, half):
        return y_part.at[a_cut[half], rows_of(peer)]

    def by_view(peer, half):
        return x_part.at[peer, b_cut[half]]

    def small_start(base, source, target, me, size, device):
        copies = []
        for k in range(1, size):
            peer = (me + k) % size
            slot = base + k - 1
            copy = remote(
                source(peer), target.at[me], s_send.at[slot], s_recv.at[slot], device(peer)
            )
            copy.start()
            copies.append(copy)
        return copies

    def small_sum(copies, target, me, own, size):
        target[me] = own
        for copy in copies:
            copy.wait_recv()
        result = target[0]
        for k in range(1, size):
            result = result + target[k]
        return result

    sy = small_start(0, lambda peer: small.at[peer], small_y, y, NY, at_y)
    ay = ring_start(ay_view, y, bufs[0], sems[0], at_y)
    bx = ring_start(bx_view, x, bufs[1], sems[1], at_x)
    ay = ring_middle(ay_view, y, bufs[0], sems[0], at_y, ay)
    bx = ring_middle(bx_view, x, bufs[1], sems[1], at_x, bx)

    hold_x[...] = small_sum(sy, small_y, y, small[y], NY)
    sx = small_start(3, lambda peer: hold_x, small_x, x, NX, at_x)

    ring_finish(ay_view, y, bufs[0], ay, y_part.at[a_cut[0]], y_part.at[a_cut[1]])
    ax = ring_start(ax_view, x, bufs[2], sems[2], at_x)
    ring_finish(
        bx_view, x, bufs[1], bx, x_part.at[pl.ds(0, 2)], x_part.at[pl.ds(2, 2)]
    )
    by = ring_start(by_view, y, bufs[3], sems[3], at_y)

    hold_z[...] = small_sum(sx, small_x, x, hold_x[...], NX)
    sz = small_start(6, lambda peer: hold_z, small_z, z, NZ, at_z)

    ax = ring_middle(ax_view, x, bufs[2], sems[2], at_x, ax)
    by = ring_middle(by_view, y, bufs[3], sems[3], at_y, by)
    ring_finish(ax_view, x, bufs[2], ax, total.at[pl.ds(0, 3)], total.at[pl.ds(3, ZA - 3)])
    ring_finish(by_view, y, bufs[3], by, total.at[pl.ds(ZA, 2)], total.at[pl.ds(ZA + 2, 1)])

    last = []
    for k in (4, 3, 5, 2, 6, 1, 7):
        peer = (z + k) % NZ
        copy = remote(
            total.at[peer], arrived.at[k - 1], z_send.at[k - 1], z_recv.at[k - 1], at_z(peer)
        )
        copy.start()
        last.append((k, copy))
    out_small[...] = small_sum(sz, small_z, z, hold_z[...], NZ)
    value = total[z]
    for k, copy in reversed(last):
        copy.wait_recv()
        value = value + arrived[k - 1]
    out[...] = value
    for copies in (sy, sx, sz, ay, bx, ax, by):
        for copy in copies:
            copy.wait_send()
    for k, copy in last:
        copy.wait_send()


def ring_buffers(half_0, half_1):
    shapes = [half_0, half_1, half_0, half_1, half_0, half_1, half_0, half_1]
    return [pltpu.VMEM(shape, F32) for shape in shapes]


def shards(sight, mapping, residual, counts, track, knots, orbit):
    shape = jax.ShapeDtypeStruct
    stations = (sight, mapping, residual, counts, track, knots)
    gathered = pl.pallas_call(
        gather_kernel,
        name="gather",
        out_shape=[shape((SATS, 3, PAR, EPOCHS), F32)]
        + [shape(a.shape, a.dtype) for a in stations],
        in_specs=[ANY] * 7,
        out_specs=[ANY] * 7,
        scratch_shapes=[
            pltpu.SemaphoreType.DMA((19,)),
            pltpu.SemaphoreType.DMA((19,)),
            pltpu.SemaphoreType.DMA,
        ],
        compiler_params=pltpu.CompilerParams(collective_id=0, has_side_effects=True),
    )(orbit, *stations)
    full, sight_b, mapping_b, residual_b, counts_b, track_b, knots_b = gathered

    big = 4 * EPOCHS
    wide = big + 128
    normal, small = pl.pallas_call(
        station_kernel,
        name="stations",
        out_shape=[shape((NY, NZ, 128, 128), F32), shape((NY, 16, 128), F32)],
        in_specs=[SMEM, SMEM] + [VMEM] * 11,
        out_specs=[VMEM, VMEM],
        scratch_shapes=[
            pltpu.VMEM((128, PAR, big), F32),
            pltpu.VMEM((128, PAR, big), F32),
            pltpu.VMEM((128, PAR, 128), F32),
            pltpu.VMEM((SLOTS, EPOCHS), F32),
            pltpu.VMEM((SLOTS, EPOCHS), F32),
            pltpu.VMEM((SLOTS, EPOCHS), F32),
            pltpu.VMEM((SLOTS, EPOCHS), F32),
            pltpu.VMEM((SLOTS, PAR, 2 * EPOCHS), F32),
            pltpu.VMEM((1024, wide), BF16),
            pltpu.VMEM((1024, wide), BF16),
            pltpu.VMEM((512, wide), BF16),
            pltpu.VMEM((512, wide), BF16),
            pltpu.VMEM((8, 128), BF16),
            pltpu.VMEM((8, 128), BF16),
        ],
        compiler_params=pltpu.CompilerParams(vmem_limit_bytes=60 * 1024 * 1024),
    )(
        track, track_b, full, sight, mapping, residual, counts, knots,
        sight_b, mapping_b, residual_b, counts_b, knots_b,
    )

    nb = NZ - ZA
    scratch = (
        ring_buffers((3, ROWS, 128), (ZA - 3, ROWS, 128))
        + ring_buffers((2, nb, COVER, 128), (2, nb, COVER, 128))
        + ring_buffers((3, COVER, 128), (ZA - 3, COVER, 128))
        + ring_buffers((2, COVER, 128), (1, COVER, 128))
        + [
            pltpu.VMEM((ZA, ROWS, 128), F32),
            pltpu.VMEM((NY, nb, COVER, 128), F32),
            pltpu.VMEM((NZ, COVER, 128), F32),
            pltpu.VMEM((NZ - 1, COVER, 128), F32),
            pltpu.VMEM((NY, 16, 128), F32),
            pltpu.VMEM((NX, 16, 128), F32),
            pltpu.VMEM((NZ, 16, 128), F32),
            pltpu.VMEM((16, 128), F32),
            pltpu.VMEM((16, 128), F32),
        ]
        + [pltpu.SemaphoreType.DMA((6,))] * 8
        + [
            pltpu.SemaphoreType.DMA((7,)),
            pltpu.SemaphoreType.DMA((7,)),
            pltpu.SemaphoreType.DMA((13,)),
            pltpu.SemaphoreType.DMA((13,)),
        ]
    )
    block, sums = pl.pallas_call(
        reduce_kernel,
        name="reduce",
        out_shape=[shape((COVER, 128), F32), shape((16, 128), F32)],
        in_specs=[VMEM, VMEM],
        out_specs=[VMEM, VMEM],
        scratch_shapes=scratch,
        compiler_params=pltpu.CompilerParams(collective_id=1, has_side_effects=True),
    )(normal, small)

    z, x, y, c = place()
    skip = x * 30 - jnp.minimum(x * 30 // 8, 10) * 8
    cross_factor = SATS / math.sqrt(512 * EPOCHS)
    factor = SATS / (512 * SLOTS * EPOCHS)
    owned = lax.dynamic_slice(block, (skip, 0), (30, ROWS)).T
    row = (y * 2 + c) * OWN + jnp.arange(ROWS, dtype=jnp.int32)[:, None] // PAR
    column = ((z * NX + x) * 30 + jnp.arange(30, dtype=jnp.int32)[None, :]) // PAR
    cross_part = jnp.where(row == column, 0.0, owned) * cross_factor
    right = sums[8, :ROWS] * factor
    blocks = jnp.transpose(sums[0:8, :ROWS].reshape(PAR, OWN, PAR), (1, 0, 2)) * factor
    return cross_part, right, blocks


def solution(mesh):
    placed = (
        P(("sta", "sat"), None, None, None),
        P(("sta", "sat"), None, None),
        P(("sta", "sat"), None, None),
        P(("sta", "sat"), None, None),
        P(("sta", "sat"), None),
        P(("sta", "sat"), None),
        P("sat", None, None, None),
    )
    return jax.shard_map(
        shards,
        mesh=mesh,
        in_specs=placed,
        out_specs=(P("sat", "sta"), P("sat"), P("sat", None, None)),
        check_vma=False,
    )
```

```python
import functools
import math

import jax
import jax.numpy as jnp
from jax import lax
from jax.experimental import pallas as pl
from jax.experimental.pallas import tpu as pltpu
from jax.sharding import PartitionSpec as P

F32 = jnp.float32
BF16 = jnp.bfloat16
MESH = pl.DeviceIdType.MESH
HIGH = lax.Precision.HIGHEST

SATS = 120
OWN = 15
PAR = 8
SLOTS = 32
EPOCHS = 256
KNOTS = 4
PRIOR = 1.0
NY = 4
NX = 4
NZ = 8
ROWS = 120
COVER = 40
CUT = 8
ZA = 5
ANY = pl.BlockSpec(memory_space=pl.ANY)
VMEM = pl.BlockSpec(memory_space=pltpu.VMEM)
SMEM = pl.BlockSpec(memory_space=pltpu.SMEM)


def place():
    sta = lax.axis_index("sta")
    sat = lax.axis_index("sat")
    return sta // NX, sta % NX, sat // 2, sat % 2


def remote(src, dst, send, recv, device):
    return pltpu.make_async_remote_copy(
        src_ref=src,
        dst_ref=dst,
        send_sem=send,
        recv_sem=recv,
        device_id=device,
        device_id_type=MESH,
    )


def greet(peers):
    barrier = pltpu.get_barrier_semaphore()
    for peer in peers:
        pl.semaphore_signal(barrier, inc=1, device_id=peer, device_id_type=MESH)
    pl.semaphore_wait(barrier, len(peers))


def halves(value):
    high = value.astype(BF16)
    low = (value - high.astype(F32)).astype(BF16)
    return high, low


def turned(a, b, precision=None):
    return lax.dot_general(
        a, b, (((1,), (1,)), ((), ())), preferred_element_type=F32, precision=precision
    )


def product(a_high, a_low, b_high, b_low):
    return turned(a_high, b_high) + turned(a_high, b_low) + turned(a_low, b_high)


def ring_start(view, me, buffers, sems, device, slots):
    far, right, left = (me + 2) % 4, (me + 1) % 4, (me + 3) % 4
    b_0, b_1, l_0, l_1, r_0, r_1 = buffers[:6]
    send, recv = sems
    plan = (
        (view(far, 0), b_0, right),
        (view(far, 1), b_1, left),
        (view(right, 1), l_1, right),
        (view(left, 0), r_0, left),
    )
    copies = []
    for slot in slots:
        src, dst, peer = plan[slot]
        copy = remote(src, dst, send.at[slot], recv.at[slot], device(peer))
        copy.start()
        copies.append(copy)
    return copies


def ring_middle(view, me, buffers, sems, device, copies):
    right, left = (me + 1) % 4, (me + 3) % 4
    b_0, b_1, l_0, l_1, r_0, r_1, s_0, s_1 = buffers
    send, recv = sems
    copies[0].wait_recv()
    s_0[...] = view(right, 0)[...] + b_0[...]
    one = remote(s_0, l_0, send.at[4], recv.at[4], device(right))
    one.start()
    copies[1].wait_recv()
    s_1[...] = view(left, 1)[...] + b_1[...]
    two = remote(s_1, r_1, send.at[5], recv.at[5], device(left))
    two.start()
    return copies + [one, two]


def ring_finish(view, me, buffers, copies, out_0, out_1):
    b_0, b_1, l_0, l_1, r_0, r_1 = buffers[:6]
    for index in (2, 3, 4, 5):
        copies[index].wait_recv()
    out_0[...] = view(me, 0)[...] + l_0[...] + r_0[...]
    out_1[...] = view(me, 1)[...] + l_1[...] + r_1[...]


def main_kernel(*refs):
    ids_a, ids_v, orbit = refs[0:3]
    mine = refs[3:8]
    out, out_small = refs[8:10]
    refs = refs[10:]
    other, refs = refs[:5], refs[5:]
    (ids_w, ids_b, full, sv, sd, st, sr, sides, crossed, f_high, f_low, u_high, u_low,
     extra, e_left, normal, own_sum, small), refs = refs[:18], refs[18:]
    bufs, refs = [refs[i * 8 : (i + 1) * 8] for i in range(4)], refs[32:]
    (y_part, x_part, total, arrived, small_y, small_x, small_z, hold_x, hold_z), refs = (
        refs[:9], refs[9:])
    g_send, g_recv, local = refs[:3]
    refs = refs[3:]
    sems = [(refs[2 * i], refs[2 * i + 1]) for i in range(4)]
    z_send, z_recv, s_send, s_recv = refs[8:]
    z, x, y, c = place()

    def at_y(peer):
        return (z * NX + x, peer * 2 + c)

    def at_x(peer):
        return (z * NX + peer, y * 2 + c)

    def at_z(peer):
        return (peer * NX + x, y * 2 + c)

    mate = (z * NX + x, y * 2 + 1 - c)
    far, right, left = (y + 2) % NY, (y + 1) % NY, (y + 3) % NY

    greet(
        [at_y((y + k) % NY) for k in range(1, NY)]
        + [at_x((x + k) % NX) for k in range(1, NX)]
        + [at_z((z + k) % NZ) for k in range(1, NZ)]
        + [mate]
    )

    head, tail = (0, CUT), (CUT, OWN - CUT)

    def base_of(chip, core):
        return (chip * 2 + core) * OWN

    def part(chip, cut):
        return full.at[pl.ds(base_of(chip, c) + cut[0], cut[1])]

    def own(cut):
        return orbit.at[pl.ds(cut[0], cut[1])]

    def go(slot, src, dst, device):
        copy = remote(src, dst, g_send.at[slot], g_recv.at[slot], device)
        copy.start()
        return copy

    right_head = go(0, own(head), part(y, head), at_y(right))
    left_tail = go(1, own(tail), part(y, tail), at_y(left))
    right_tail = go(2, own(tail), part(y, tail), at_y(right))
    left_head = go(3, own(head), part(y, head), at_y(left))
    keep = pltpu.make_async_copy(orbit, full.at[pl.ds(base_of(y, c), OWN)], local.at[0])
    keep.start()
    swaps = [go(6 + i, a, b, mate) for i, (a, b) in enumerate(zip((ids_v,) + mine, (ids_w,) + other))]
    mate_own = go(12, orbit, full.at[pl.ds(base_of(y, c), OWN)], mate)

    extra[...] = jnp.zeros_like(extra)
    sv[:, :, SLOTS:, :] = jnp.zeros((4, 3, 8, EPOCHS), F32)
    sd[:, :, SLOTS:, :] = jnp.zeros((4, 3, 8, EPOCHS), F32)
    crossed[:, SLOTS:] = jnp.zeros((4, 8, PAR, 128), F32)
    lane_rows = lax.broadcasted_iota(jnp.int32, (128, EPOCHS), 0)
    row8 = lax.broadcasted_iota(jnp.int32, (8, EPOCHS), 0)

    def knot_rows(index):
        knots = mine[4] if index < 2 else other[4]
        pick = lane_rows % 32 == knots[index % 2 : index % 2 + 1, :] + KNOTS * index
        return jnp.where(pick & (lane_rows < 96), 1.0, 0.0)

    def prepare(index):
        sight, mapping, residual, counts, _ = mine if index < 2 else other
        s = index % 2
        weight = counts[s].astype(F32)
        path = mapping[s]
        seen = residual[s]
        shared = jnp.maximum(jnp.sum(weight, 0, keepdims=True), 1.0)
        share = 1.0 / shared
        weight_map = weight * path
        sum_map = jnp.sum(weight_map, 0, keepdims=True)
        sum_res = jnp.sum(weight * seen, 0, keepdims=True)
        st[index] = weight * (path - sum_map * share)
        sr[index] = weight * (seen - sum_res * share)
        root = weight * lax.rsqrt(shared)
        other_root = jnp.sqrt(weight)
        for k in range(3):
            sv[index, k, 0:SLOTS] = sight[s, k] * root
            sd[index, k, 0:SLOTS] = sight[s, k] * other_root
        square = jnp.sum(weight_map * path, 0, keepdims=True) - sum_map * sum_map * share
        cross = jnp.sum(weight_map * seen, 0, keepdims=True) - sum_map * sum_res * share
        pair = jnp.where(row8 == 0, square, jnp.where(row8 == 1, cross, 0.0))
        return turned(pair, knot_rows(index), HIGH)

    own_row = lax.broadcasted_iota(jnp.int32, (128, 128), 0) // PAR
    own_lane = lax.broadcasted_iota(jnp.int32, (128, 128), 1) // PAR

    def squeeze(block):
        block = jnp.where(own_row == own_lane, block, 0.0)
        return jnp.sum(block.reshape(16, PAR, 128), 0)

    def build(chip, core, diagonal):
        base = base_of(chip, core)
        top = (chip * 2 + core) * 128

        def one(j, index, table):
            ids = ids_a if index < 2 else ids_b
            slot = ids[index % 2, base + j]
            return (
                table[index, 0, pl.ds(slot, 1), :] * full[base + j, 0]
                + table[index, 1, pl.ds(slot, 1), :] * full[base + j, 1]
                + table[index, 2, pl.ds(slot, 1), :] * full[base + j, 2]
            )

        def fill(k, second):
            row = pl.multiple_of(top + k * 16, 16)
            inner = pl.multiple_of(k * 16, 16)
            for index in range(4):
                lanes = slice(index * EPOCHS, (index + 1) * EPOCHS)
                a = one(2 * k, index, sv)
                b = one(2 * k + 1, index, sv) if second else jnp.zeros_like(a)
                high, low = halves(jnp.concatenate([a, b], axis=0))
                f_high[pl.ds(row, 16), lanes] = high
                f_low[pl.ds(row, 16), lanes] = low
                if diagonal:
                    a = one(2 * k, index, sd)
                    b = one(2 * k + 1, index, sd) if second else jnp.zeros_like(a)
                    high, low = halves(jnp.concatenate([a, b], axis=0))
                    u_high[pl.ds(inner, 16), lanes] = high
                    u_low[pl.ds(inner, 16), lanes] = low

        def step(k, carry):
            fill(k, True)
            return carry

        lax.fori_loop(0, 7, step, 0)
        fill(7, False)
        if diagonal:
            own_sum[chip] = squeeze(product(u_high[...], u_low[...], u_high[...], u_low[...]))

    local_rows = prepare(0) + prepare(1)
    keep.wait()
    for copy in swaps:
        copy.wait_recv()
    hand = pltpu.make_async_copy(ids_w, ids_b, local.at[1])
    hand.start()
    local_rows = local_rows + prepare(2) + prepare(3)
    hand.wait()
    build(y, c, True)
    mates = [mate_own]
    right_head.wait_recv()
    relay_right = go(4, part(left, head), part(left, head), at_y(right))
    mates.append(go(13, part(left, head), part(left, head), mate))
    left_tail.wait_recv()
    relay_left = go(5, part(right, tail), part(right, tail), at_y(left))
    mates.append(go(14, part(right, tail), part(right, tail), mate))
    mate_own.wait_recv()
    build(y, 1 - c, False)
    right_tail.wait_recv()
    mates.append(go(15, part(left, tail), part(left, tail), mate))
    left_head.wait_recv()
    mates.append(go(16, part(right, head), part(right, head), mate))
    build(left, c, True)
    build(right, c, True)
    for copy in mates[1:]:
        copy.wait_recv()
    build(left, 1 - c, False)
    build(right, 1 - c, False)
    relay_right.wait_recv()
    mates.append(go(17, part(far, head), part(far, head), mate))
    relay_left.wait_recv()
    mates.append(go(18, part(far, tail), part(far, tail), mate))
    build(far, c, True)
    for copy in mates[5:]:
        copy.wait_recv()
    build(far, 1 - c, False)

    for index in range(4):
        sight = mine[0] if index < 2 else other[0]
        ids = ids_a if index < 2 else ids_b
        s = index % 2

        def visit(m, carry):
            sat = ids[2 + s, m]
            design = (
                sight[s, 0, pl.ds(m, 1), :] * full[sat, 0]
                + sight[s, 1, pl.ds(m, 1), :] * full[sat, 1]
                + sight[s, 2, pl.ds(m, 1), :] * full[sat, 2]
            )
            sides[m, :, 0:EPOCHS] = design * st[index, pl.ds(m, 1), :]
            sides[m, :, EPOCHS : 2 * EPOCHS] = design * sr[index, pl.ds(m, 1), :]
            return carry

        lax.fori_loop(0, SLOTS, visit, 0, unroll=4)
        high, low = halves(sides[...].reshape(SLOTS * PAR, 2 * EPOCHS))
        last_rows = jnp.where((lane_rows % 32 == 16) & (lane_rows < 96), 1.0, 0.0)
        pickers = jnp.concatenate([knot_rows(index), last_rows], axis=1).astype(BF16)
        crossed[index, 0:SLOTS] = (turned(high, pickers) + turned(low, pickers)).reshape(
            SLOTS, PAR, 128
        )

    def collect(group, carry):
        for j in range(OWN):
            sat = group * OWN + j
            extra[group * 16 + j] = (
                crossed[0, ids_a[0, sat]]
                + crossed[1, ids_a[1, sat]]
                + crossed[2, ids_b[0, sat]]
                + crossed[3, ids_b[1, sat]]
            )
        return carry

    lax.fori_loop(0, NZ, collect, 0)

    lane = lax.broadcasted_iota(jnp.int32, (1, 128), 1)
    scale = jnp.where(lane % 32 < 16, lax.rsqrt(local_rows[0:1] + PRIOR), 0.0)
    special = jnp.where(lane % 32 == 16, -1.0, local_rows[1:2] * scale)
    row = lax.broadcasted_iota(jnp.int32, (8, 128), 0)
    left_scale = jnp.broadcast_to(scale, (1024, 128))
    side = extra[...].reshape(1024, 128) * left_scale
    high, low = halves(side)
    e_left[...] = jnp.where(lane < 64, high.astype(F32), low.astype(F32)).astype(BF16)
    special = jnp.where(row == 0, special, 0.0)
    high, low = halves(special)
    special = jnp.where(lane < 64, high.astype(F32), low.astype(F32))
    e_left[112:128] = jnp.concatenate(
        [e_left[112:128].astype(F32)[0:8], special], axis=0
    ).astype(BF16)
    right_scale = jnp.where(lane % 32 < 16, scale, 1.0)

    def right_side(slab):
        group = slab * 2 + c
        rows = pl.ds(pl.multiple_of(group * 128, 128), 128)
        side = extra[pl.ds(group * 16, 16)].reshape(128, 128) * right_scale
        high, low = halves(side)
        side = jnp.where((lane >= 32) & (lane < 64), low.astype(F32), high.astype(F32))
        return f_high[rows], f_low[rows], side.astype(BF16)

    def multiply(first, count, slabs):
        rows = slice(first * 128, (first + count) * 128)
        sides_of = [right_side(slab) for slab in slabs]
        r_high, r_low, r_side = [
            jnp.concatenate([part[i] for part in sides_of], axis=0) for i in range(3)
        ]
        result = product(f_high[rows], f_low[rows], r_high, r_low) + turned(e_left[rows], r_side)
        for i, slab in enumerate(slabs):
            lanes = slice(i * 128, (i + 1) * 128)
            normal[slab, first : first + count] = -result[:, lanes].reshape(count, 128, 128)

    def rows_of(peer):
        return pl.ds(pl.multiple_of(jnp.minimum(peer * 30 // 8, 10) * 8, 8), COVER)

    a_cut = (pl.ds(0, 3), pl.ds(3, ZA - 3))
    b_cut = (pl.ds(0, 2), pl.ds(2, 1))

    def ay_view(peer, half):
        return normal.at[peer, a_cut[half], pl.ds(0, ROWS)]

    def bx_view(peer, half):
        return normal.at[pl.ds(2 * half, 2), pl.ds(ZA, NZ - ZA), rows_of(peer)]

    def ax_view(peer, half):
        return y_part.at[a_cut[half], rows_of(peer)]

    def by_view(peer, half):
        return x_part.at[peer, b_cut[half]]

    def small_start(base, source, target, me, size, device):
        copies = []
        for k in range(1, size):
            peer = (me + k) % size
            slot = base + k - 1
            copy = remote(
                source(peer), target.at[me], s_send.at[slot], s_recv.at[slot], device(peer)
            )
            copy.start()
            copies.append(copy)
        return copies

    def small_sum(copies, target, me, own, size):
        target[me] = own
        for copy in copies:
            copy.wait_recv()
        result = target[0]
        for k in range(1, size):
            result = result + target[k]
        return result

    multiply(0, 3, (far, right))
    ay = ring_start(ay_view, y, bufs[0], sems[0], at_y, (0,))
    multiply(3, ZA - 3, (far, right))
    ay += ring_start(ay_view, y, bufs[0], sems[0], at_y, (1, 2))
    multiply(ZA, NZ - ZA, (far, right))
    multiply(ZA, NZ - ZA, (left, y))
    bx = ring_start(bx_view, x, bufs[1], sems[1], at_x, (0, 1, 2, 3))
    multiply(0, 3, (left, y))
    ay += ring_start(ay_view, y, bufs[0], sems[0], at_y, (3,))
    multiply(3, ZA - 3, (left, y))

    for slab in range(NY):
        small[slab, 0:8] = own_sum[slab] + squeeze(normal[slab, slab * 2 + c])
        small[slab, 8:16] = normal[slab, 0, ROWS : ROWS + 8, :]
    sy = small_start(0, lambda peer: small.at[peer], small_y, y, NY, at_y)

    ay = ring_middle(ay_view, y, bufs[0], sems[0], at_y, ay)
    bx = ring_middle(bx_view, x, bufs[1], sems[1], at_x, bx)

    hold_x[...] = small_sum(sy, small_y, y, small[y], NY)
    sx = small_start(3, lambda peer: hold_x, small_x, x, NX, at_x)

    ring_finish(ay_view, y, bufs[0], ay, y_part.at[a_cut[0]], y_part.at[a_cut[1]])
    ax = ring_start(ax_view, x, bufs[2], sems[2], at_x, (0, 1, 2, 3))
    ring_finish(
        bx_view, x, bufs[1], bx, x_part.at[pl.ds(0, 2)], x_part.at[pl.ds(2, 2)]
    )
    by = ring_start(by_view, y, bufs[3], sems[3], at_y, (0, 1, 2, 3))

    hold_z[...] = small_sum(sx, small_x, x, hold_x[...], NX)
    sz = small_start(6, lambda peer: hold_z, small_z, z, NZ, at_z)

    ax = ring_middle(ax_view, x, bufs[2], sems[2], at_x, ax)
    by = ring_middle(by_view, y, bufs[3], sems[3], at_y, by)
    ring_finish(ax_view, x, bufs[2], ax, total.at[pl.ds(0, 3)], total.at[pl.ds(3, ZA - 3)])
    ring_finish(by_view, y, bufs[3], by, total.at[pl.ds(ZA, 2)], total.at[pl.ds(ZA + 2, 1)])

    final = []
    for k in (4, 3, 5, 2, 6, 1, 7):
        peer = (z + k) % NZ
        copy = remote(
            total.at[peer], arrived.at[k - 1], z_send.at[k - 1], z_recv.at[k - 1], at_z(peer)
        )
        copy.start()
        final.append((k, copy))
    out_small[...] = small_sum(sz, small_z, z, hold_z[...], NZ)
    value = total[z]
    for k, copy in reversed(final):
        copy.wait_recv()
        value = value + arrived[k - 1]
    out[...] = value
    sent = [right_head, left_tail, right_tail, left_head, relay_right, relay_left]
    for copies in (sent, swaps, mates, sy, sx, sz, ay, bx, ax, by):
        for copy in copies:
            copy.wait_send()
    for k, copy in final:
        copy.wait_send()


def finish_kernel(block, sums, owned, right, blocks):
    z, x, y, c = place()
    skip = x * 30 - jnp.minimum(x * 30 // 8, 10) * 8
    cross_factor = SATS / math.sqrt(512 * EPOCHS)
    factor = SATS / (512 * SLOTS * EPOCHS)
    value = pltpu.roll(block[...], COVER - skip, 0)[0:30, 0:ROWS]
    row = (z * NX + x) * 30 + lax.broadcasted_iota(jnp.int32, (30, ROWS), 0)
    column = (y * 2 + c) * ROWS + lax.broadcasted_iota(jnp.int32, (30, ROWS), 1)
    owned[...] = jnp.where(row // PAR == column // PAR, 0.0, value) * cross_factor
    right[...] = sums[8:9, 0:ROWS] * factor
    scaled = sums[0:8] * factor
    for j in range(OWN):
        blocks[j] = scaled[:, j * PAR : (j + 1) * PAR]


def ring_buffers(half_0, half_1):
    shapes = [half_0, half_1, half_0, half_1, half_0, half_1, half_0, half_1]
    return [pltpu.VMEM(shape, F32) for shape in shapes]


def shards(sight, mapping, residual, counts, track, knots, orbit):
    shape = jax.ShapeDtypeStruct
    stations = (sight, mapping, residual, counts, knots)
    hit = track[:, :, None] == jnp.arange(128, dtype=jnp.int32)[None, None, :]
    offset = jnp.arange(SLOTS, dtype=jnp.int32)[None, :, None] - SLOTS
    slots = SLOTS + jnp.sum(jnp.where(hit, offset, 0), axis=1)
    ids = jnp.concatenate([slots, jnp.pad(track, ((0, 0), (0, 128 - SLOTS)))], axis=0)

    nb = NZ - ZA
    scratch = (
        [pltpu.VMEM(a.shape, a.dtype) for a in stations]
        + [
            pltpu.VMEM((4, 128), jnp.int32),
            pltpu.SMEM((4, 128), jnp.int32),
            pltpu.VMEM((SATS, 3, PAR, EPOCHS), F32),
            pltpu.VMEM((4, 3, SLOTS + 8, EPOCHS), F32),
            pltpu.VMEM((4, 3, SLOTS + 8, EPOCHS), F32),
            pltpu.VMEM((4, SLOTS, EPOCHS), F32),
            pltpu.VMEM((4, SLOTS, EPOCHS), F32),
            pltpu.VMEM((SLOTS, PAR, 2 * EPOCHS), F32),
            pltpu.VMEM((4, SLOTS + 8, PAR, 128), F32),
            pltpu.VMEM((1024, 4 * EPOCHS), BF16),
            pltpu.VMEM((1024, 4 * EPOCHS), BF16),
            pltpu.VMEM((128, 4 * EPOCHS), BF16),
            pltpu.VMEM((128, 4 * EPOCHS), BF16),
            pltpu.VMEM((128, PAR, 128), F32),
            pltpu.VMEM((1024, 128), BF16),
            pltpu.VMEM((NY, NZ, 128, 128), F32),
            pltpu.VMEM((NY, PAR, 128), F32),
            pltpu.VMEM((NY, 16, 128), F32),
        ]
        + ring_buffers((3, ROWS, 128), (ZA - 3, ROWS, 128))
        + ring_buffers((2, nb, COVER, 128), (2, nb, COVER, 128))
        + ring_buffers((3, COVER, 128), (ZA - 3, COVER, 128))
        + ring_buffers((2, COVER, 128), (1, COVER, 128))
        + [
            pltpu.VMEM((ZA, ROWS, 128), F32),
            pltpu.VMEM((NY, nb, COVER, 128), F32),
            pltpu.VMEM((NZ, COVER, 128), F32),
            pltpu.VMEM((NZ - 1, COVER, 128), F32),
            pltpu.VMEM((NY, 16, 128), F32),
            pltpu.VMEM((NX, 16, 128), F32),
            pltpu.VMEM((NZ, 16, 128), F32),
            pltpu.VMEM((16, 128), F32),
            pltpu.VMEM((16, 128), F32),
            pltpu.SemaphoreType.DMA((19,)),
            pltpu.SemaphoreType.DMA((19,)),
            pltpu.SemaphoreType.DMA((2,)),
        ]
        + [pltpu.SemaphoreType.DMA((6,))] * 8
        + [
            pltpu.SemaphoreType.DMA((7,)),
            pltpu.SemaphoreType.DMA((7,)),
            pltpu.SemaphoreType.DMA((13,)),
            pltpu.SemaphoreType.DMA((13,)),
        ]
    )
    block, sums = pl.pallas_call(
        main_kernel,
        name="network",
        out_shape=[shape((COVER, 128), F32), shape((16, 128), F32)],
        in_specs=[SMEM] + [VMEM] * 7,
        out_specs=[VMEM, VMEM],
        scratch_shapes=scratch,
        compiler_params=pltpu.CompilerParams(
            collective_id=0, has_side_effects=True, vmem_limit_bytes=60 * 1024 * 1024
        ),
    )(ids, ids, orbit, *stations)

    owned, right, blocks = pl.pallas_call(
        finish_kernel,
        name="finish",
        out_shape=[
            shape((30, ROWS), F32),
            shape((1, ROWS), F32),
            shape((OWN, PAR, PAR), F32),
        ],
        in_specs=[VMEM, VMEM],
        out_specs=[VMEM] * 3,
    )(block, sums)
    return owned.T, right.reshape(ROWS), blocks


def solution(mesh):
    placed = (
        P(("sta", "sat"), None, None, None),
        P(("sta", "sat"), None, None),
        P(("sta", "sat"), None, None),
        P(("sta", "sat"), None, None),
        P(("sta", "sat"), None),
        P(("sta", "sat"), None),
        P("sat", None, None, None),
    )
    return jax.shard_map(
        shards,
        mesh=mesh,
        in_specs=placed,
        out_specs=(P("sat", "sta"), P("sat"), P("sat", None, None)),
        check_vma=False,
    )
```

```python
import functools
import math

import jax
import jax.numpy as jnp
from jax import lax
from jax.experimental import pallas as pl
from jax.experimental.pallas import tpu as pltpu
from jax.sharding import PartitionSpec as P

F32 = jnp.float32
BF16 = jnp.bfloat16
MESH = pl.DeviceIdType.MESH
HIGH = lax.Precision.HIGHEST

SATS = 120
OWN = 15
PAR = 8
SLOTS = 32
EPOCHS = 256
KNOTS = 4
PRIOR = 1.0
NY = 4
NX = 4
NZ = 8
ROWS = 120
COVER = 40
CUT = 8
ZA = 5
ANY = pl.BlockSpec(memory_space=pl.ANY)
VMEM = pl.BlockSpec(memory_space=pltpu.VMEM)
SMEM = pl.BlockSpec(memory_space=pltpu.SMEM)


def place():
    sta = lax.axis_index("sta")
    sat = lax.axis_index("sat")
    return sta // NX, sta % NX, sat // 2, sat % 2


def remote(src, dst, send, recv, device):
    return pltpu.make_async_remote_copy(
        src_ref=src,
        dst_ref=dst,
        send_sem=send,
        recv_sem=recv,
        device_id=device,
        device_id_type=MESH,
    )


def greet(peers):
    barrier = pltpu.get_barrier_semaphore()
    for peer in peers:
        pl.semaphore_signal(barrier, inc=1, device_id=peer, device_id_type=MESH)
    pl.semaphore_wait(barrier, len(peers))


def halves(value):
    high = value.astype(BF16)
    low = (value - high.astype(F32)).astype(BF16)
    return high, low


def turned(a, b, precision=None):
    return lax.dot_general(
        a, b, (((1,), (1,)), ((), ())), preferred_element_type=F32, precision=precision
    )


def product(a_high, a_low, b_high, b_low):
    return turned(a_high, b_high) + turned(a_high, b_low) + turned(a_low, b_high)


def ring_start(view, me, buffers, sems, device, slots):
    far, right, left = (me + 2) % 4, (me + 1) % 4, (me + 3) % 4
    b_0, b_1, l_0, l_1, r_0, r_1 = buffers[:6]
    send, recv = sems
    plan = (
        (view(far, 0), b_0, right),
        (view(far, 1), b_1, left),
        (view(right, 1), l_1, right),
        (view(left, 0), r_0, left),
    )
    copies = []
    for slot in slots:
        src, dst, peer = plan[slot]
        copy = remote(src, dst, send.at[slot], recv.at[slot], device(peer))
        copy.start()
        copies.append(copy)
    return copies


def ring_middle(view, me, buffers, sems, device, copies):
    right, left = (me + 1) % 4, (me + 3) % 4
    b_0, b_1, l_0, l_1, r_0, r_1, s_0, s_1 = buffers
    send, recv = sems
    copies[0].wait_recv()
    s_0[...] = view(right, 0)[...] + b_0[...]
    one = remote(s_0, l_0, send.at[4], recv.at[4], device(right))
    one.start()
    copies[1].wait_recv()
    s_1[...] = view(left, 1)[...] + b_1[...]
    two = remote(s_1, r_1, send.at[5], recv.at[5], device(left))
    two.start()
    return copies + [one, two]


def ring_finish(view, me, buffers, copies, out_0, out_1):
    b_0, b_1, l_0, l_1, r_0, r_1 = buffers[:6]
    for index in (2, 3, 4, 5):
        copies[index].wait_recv()
    out_0[...] = view(me, 0)[...] + l_0[...] + r_0[...]
    out_1[...] = view(me, 1)[...] + l_1[...] + r_1[...]


def main_kernel(*refs):
    track, orbit = refs[0:2]
    given = refs[2:7]
    out, out_small = refs[7:9]
    refs = refs[9:]
    mine, other, refs = refs[:5], refs[5:10], refs[10:]
    (track_s, ids_v, ids_w, ids_a, ids_b, full, sv, factors, f_high, f_low, u_high, u_low,
     t_high, t_low, pick, e_left, e_right, normal, own_sum, small), refs = refs[:20], refs[20:]
    bufs, refs = [refs[i * 8 : (i + 1) * 8] for i in range(6)], refs[48:]
    (y_part, x_part, total, arrived, small_y, small_x, small_z, hold_x, hold_z), refs = (
        refs[:9], refs[9:])
    g_send, g_recv, local = refs[:3]
    refs = refs[3:]
    sems = [(refs[2 * i], refs[2 * i + 1]) for i in range(6)]
    z_send, z_recv, s_send, s_recv = refs[12:]
    z, x, y, c = place()

    def at_y(peer):
        return (z * NX + x, peer * 2 + c)

    def at_x(peer):
        return (z * NX + peer, y * 2 + c)

    def at_z(peer):
        return (peer * NX + x, y * 2 + c)

    mate = (z * NX + x, y * 2 + 1 - c)
    far, right, left = (y + 2) % NY, (y + 1) % NY, (y + 3) % NY
    head, tail = (0, CUT), (CUT, OWN - CUT)

    def base_of(chip, core):
        return (chip * 2 + core) * OWN

    def part(chip, cut):
        return full.at[pl.ds(base_of(chip, c) + cut[0], cut[1])]

    def own(cut):
        return orbit.at[pl.ds(cut[0], cut[1])]

    keeps = [
        pltpu.make_async_copy(a, b, local.at[i])
        for i, (a, b) in enumerate(
            zip(
                (track,) + given + (orbit,),
                (track_s,) + mine + (full.at[pl.ds(base_of(y, c), OWN)],),
            )
        )
    ]
    for copy in keeps:
        copy.start()

    greet(
        [at_y((y + k) % NY) for k in range(1, NY)]
        + [at_x((x + k) % NX) for k in range(1, NX)]
        + [at_z((z + k) % NZ) for k in range(1, NZ)]
        + [mate]
    )

    def go(slot, src, dst, device):
        copy = remote(src, dst, g_send.at[slot], g_recv.at[slot], device)
        copy.start()
        return copy

    right_head = go(0, own(head), part(y, head), at_y(right))
    left_tail = go(1, own(tail), part(y, tail), at_y(left))
    right_tail = go(2, own(tail), part(y, tail), at_y(right))
    left_head = go(3, own(head), part(y, head), at_y(left))
    swaps = [go(7 + i, a, b, mate) for i, (a, b) in enumerate(zip(given, other))]
    mate_own = go(12, orbit, full.at[pl.ds(base_of(y, c), OWN)], mate)

    keeps[0].wait()
    place_lane = lax.broadcasted_iota(jnp.int32, (1, 128), 1)
    for s in range(2):
        slots = jnp.full((1, 128), SLOTS, jnp.int32)
        for m in range(SLOTS):
            slots = jnp.where(place_lane == track_s[s, m], m, slots)
        ids_v[s : s + 1, :] = slots
    hand_a = pltpu.make_async_copy(ids_v, ids_a, local.at[7])
    hand_a.start()
    swaps.append(go(6, ids_v, ids_w, mate))

    blank = jnp.zeros((4, 3, 8, EPOCHS), F32)
    sv[:, :, SLOTS:, :] = blank
    factors[:, :, SLOTS:, :] = blank
    lane_rows = lax.broadcasted_iota(jnp.int32, (128, EPOCHS), 0)
    row8 = lax.broadcasted_iota(jnp.int32, (8, EPOCHS), 0)
    pick_last = jnp.where((lane_rows % 32 == 16) & (lane_rows < 96), 1.0, 0.0).astype(BF16)

    def prepare(index):
        sight, mapping, residual, counts, knots = mine if index < 2 else other
        s = index % 2
        chosen = lane_rows % 32 == knots[s : s + 1, :] + KNOTS * index
        chosen = jnp.where(chosen & (lane_rows < 96), 1.0, 0.0)
        wide = 2 * EPOCHS * index
        pick[:, wide : wide + EPOCHS] = chosen.astype(BF16)
        pick[:, wide + EPOCHS : wide + 2 * EPOCHS] = pick_last
        weight = counts[s].astype(F32)
        path = mapping[s]
        seen = residual[s]
        shared = jnp.maximum(jnp.sum(weight, 0, keepdims=True), 1.0)
        share = 1.0 / shared
        root = lax.rsqrt(shared)
        grow = shared * root
        weight_map = weight * path
        sum_map = jnp.sum(weight_map, 0, keepdims=True)
        sum_res = jnp.sum(weight * seen, 0, keepdims=True)
        scaled = weight * root
        for k in range(3):
            sv[index, k, 0:SLOTS] = sight[s, k] * scaled
        factors[index, 0, 0:SLOTS] = jnp.where(
            weight > 0.0, lax.rsqrt(jnp.maximum(weight, 1.0)) * grow, 0.0
        )
        factors[index, 1, 0:SLOTS] = (path - sum_map * share) * grow
        factors[index, 2, 0:SLOTS] = (seen - sum_res * share) * grow
        square = jnp.sum(weight_map * path, 0, keepdims=True) - sum_map * sum_map * share
        cross = jnp.sum(weight_map * seen, 0, keepdims=True) - sum_map * sum_res * share
        pair = jnp.where(row8 == 0, square, jnp.where(row8 == 1, cross, 0.0))
        return turned(pair, chosen, HIGH)

    own_row = lax.broadcasted_iota(jnp.int32, (128, 128), 0) // PAR
    own_lane = lax.broadcasted_iota(jnp.int32, (128, 128), 1) // PAR
    lane = lax.broadcasted_iota(jnp.int32, (1, 128), 1)

    def squeeze(block):
        block = jnp.where(own_row == own_lane, block, 0.0)
        return jnp.sum(block.reshape(16, PAR, 128), 0)

    def build(chip, core, sides, diagonal):
        base = base_of(chip, core)
        group = chip * 2 + core
        top = group * 128

        def one(j, index):
            ids = ids_a if index < 2 else ids_b
            slot = ids[index % 2, base + j]
            value = (
                sv[index, 0, pl.ds(slot, 1), :] * full[base + j, 0]
                + sv[index, 1, pl.ds(slot, 1), :] * full[base + j, 1]
                + sv[index, 2, pl.ds(slot, 1), :] * full[base + j, 2]
            )
            times = [
                value * factors[index, k, pl.ds(slot, 1), :]
                for k in range(3)
                if (diagonal if k == 0 else sides)
            ]
            return [value] + times

        def fill(k, second):
            row = pl.multiple_of(top + k * 16, 16)
            inner = pl.multiple_of(k * 16, 16)
            for index in range(4):
                lanes = slice(index * EPOCHS, (index + 1) * EPOCHS)
                a = one(2 * k, index)
                b = one(2 * k + 1, index) if second else [jnp.zeros_like(i) for i in a]
                pieces = [halves(jnp.concatenate([i, j], axis=0)) for i, j in zip(a, b)]
                if sides:
                    f_high[pl.ds(row, 16), lanes], f_low[pl.ds(row, 16), lanes] = pieces[0]
                if diagonal:
                    u_high[pl.ds(inner, 16), lanes], u_low[pl.ds(inner, 16), lanes] = pieces[1]
                if sides:
                    wide = 2 * EPOCHS * index
                    for i in range(2):
                        lanes = slice(wide + i * EPOCHS, wide + (i + 1) * EPOCHS)
                        high, low = pieces[i - 2]
                        t_high[pl.ds(inner, 16), lanes] = high
                        t_low[pl.ds(inner, 16), lanes] = low

        def step(k, carry):
            fill(k, True)
            return carry

        lax.fori_loop(0, 7, step, 0)
        fill(7, False)
        if sides:
            side = turned(t_high[...], pick[...]) + turned(t_low[...], pick[...])
            rows = pl.ds(pl.multiple_of(top, 128), 128)
            high, low = halves(side * scale)
            high, low = high.astype(F32), low.astype(F32)
            e_left[rows] = jnp.where(lane < 64, high, low).astype(BF16)
            high, low = halves(side * right_scale)
            high, low = high.astype(F32), low.astype(F32)
            e_right[rows] = jnp.where((lane >= 32) & (lane < 64), low, high).astype(BF16)
        if diagonal:
            own_sum[chip] = squeeze(product(u_high[...], u_low[...], u_high[...], u_low[...]))

    for copy in keeps[1:]:
        copy.wait()
    hand_a.wait()
    local_rows = prepare(0) + prepare(1)
    for copy in swaps:
        copy.wait_recv()
    hand_b = pltpu.make_async_copy(ids_w, ids_b, local.at[8])
    hand_b.start()
    local_rows = local_rows + prepare(2) + prepare(3)
    scale = jnp.where(lane % 32 < 16, lax.rsqrt(local_rows[0:1] + PRIOR), 0.0)
    right_scale = jnp.where(lane % 32 < 16, scale, 1.0)
    special = jnp.where(lane % 32 == 16, -1.0, local_rows[1:2] * scale)
    hand_b.wait()
    build(y, c, True, True)
    mates = [mate_own]
    right_head.wait_recv()
    relay_right = go(4, part(left, head), part(left, head), at_y(right))
    mates.append(go(13, part(left, head), part(left, head), mate))
    left_tail.wait_recv()
    relay_left = go(5, part(right, tail), part(right, tail), at_y(left))
    mates.append(go(14, part(right, tail), part(right, tail), mate))
    mate_own.wait_recv()
    build(y, 1 - c, True, False)
    right_tail.wait_recv()
    mates.append(go(15, part(left, tail), part(left, tail), mate))
    left_head.wait_recv()
    mates.append(go(16, part(right, head), part(right, head), mate))
    build(left, c, True, True)
    build(right, c, True, True)
    for copy in mates[1:]:
        copy.wait_recv()
    build(left, 1 - c, True, False)
    build(right, 1 - c, True, False)
    relay_right.wait_recv()
    mates.append(go(17, part(far, head), part(far, head), mate))
    relay_left.wait_recv()
    mates.append(go(18, part(far, tail), part(far, tail), mate))
    build(far, c, True, False)
    for copy in mates[5:]:
        copy.wait_recv()
    build(far, 1 - c, True, False)

    row = lax.broadcasted_iota(jnp.int32, (8, 128), 0)
    high, low = halves(jnp.where(row == 0, special, 0.0))
    special = jnp.where(lane < 64, high.astype(F32), low.astype(F32))
    e_left[112:128] = jnp.concatenate(
        [e_left[112:128].astype(F32)[0:8], special], axis=0
    ).astype(BF16)

    def multiply(first, count, slabs):
        rows = slice(first * 128, (first + count) * 128)
        own_rows = [pl.ds(pl.multiple_of((slab * 2 + c) * 128, 128), 128) for slab in slabs]
        r_high, r_low, r_side = [
            jnp.concatenate([ref[i] for i in own_rows], axis=0)
            for ref in (f_high, f_low, e_right)
        ]
        result = product(f_high[rows], f_low[rows], r_high, r_low) + turned(e_left[rows], r_side)
        for i, slab in enumerate(slabs):
            lanes = slice(i * 128, (i + 1) * 128)
            normal[slab, first : first + count] = -result[:, lanes].reshape(count, 128, 128)

    def rows_of(peer):
        return pl.ds(pl.multiple_of(jnp.minimum(peer * 30 // 8, 10) * 8, 8), COVER)

    row_cut = (pl.ds(0, 64), pl.ds(64, ROWS - 64))
    cuts = ((pl.ds(0, 2), pl.ds(2, 1)), (pl.ds(3, 1), pl.ds(4, 1)))
    b_cut = (pl.ds(0, 2), pl.ds(2, 1))

    def first_view(which):
        zs = (pl.ds(0, 3), pl.ds(3, 2))[which]
        return lambda peer, half: normal.at[peer, zs, row_cut[half]]

    def second_view(which):
        return lambda peer, half: y_part.at[cuts[which][half], rows_of(peer)]

    def bx_view(peer, half):
        return normal.at[pl.ds(2 * half, 2), pl.ds(ZA, NZ - ZA), rows_of(peer)]

    def by_view(peer, half):
        return x_part.at[peer, b_cut[half]]

    def small_start(base, source, target, me, size, device):
        copies = []
        for k in range(1, size):
            peer = (me + k) % size
            slot = base + k - 1
            copy = remote(
                source(peer), target.at[me], s_send.at[slot], s_recv.at[slot], device(peer)
            )
            copy.start()
            copies.append(copy)
        return copies

    def small_sum(copies, target, me, own, size):
        target[me] = own
        for copy in copies:
            copy.wait_recv()
        result = target[0]
        for k in range(1, size):
            result = result + target[k]
        return result

    def last_copy(peer, slot):
        return remote(
            total.at[peer], arrived.at[slot], z_send.at[peer], z_recv.at[slot], at_z(peer)
        )

    def send_last(peers):
        for peer in peers:
            @pl.when(z != peer)
            def _():
                last_copy(peer, z).start()

    a_1, a_2 = first_view(0), first_view(1)
    multiply(0, 3, (far, right))
    ay_1 = ring_start(a_1, y, bufs[0], sems[0], at_y, (0, 1, 2))
    multiply(3, 2, (far, right))
    ay_2 = ring_start(a_2, y, bufs[1], sems[1], at_y, (0, 1, 2))
    multiply(ZA, NZ - ZA, (far, right))
    multiply(ZA, NZ - ZA, (left, y))
    bx = ring_start(bx_view, x, bufs[2], sems[2], at_x, (0, 1, 2, 3))
    multiply(0, 3, (left, y))
    ay_1 += ring_start(a_1, y, bufs[0], sems[0], at_y, (3,))
    multiply(3, 2, (left, y))
    ay_2 += ring_start(a_2, y, bufs[1], sems[1], at_y, (3,))
    ay_1 = ring_middle(a_1, y, bufs[0], sems[0], at_y, ay_1)

    build(far, c, False, True)
    for slab in range(NY):
        small[slab, 0:8] = own_sum[slab] + squeeze(normal[slab, slab * 2 + c])
        small[slab, 8:16] = normal[slab, 0, ROWS : ROWS + 8, :]
    sy = small_start(0, lambda peer: small.at[peer], small_y, y, NY, at_y)

    ay_2 = ring_middle(a_2, y, bufs[1], sems[1], at_y, ay_2)
    bx = ring_middle(bx_view, x, bufs[2], sems[2], at_x, bx)

    c_1, c_2 = second_view(0), second_view(1)
    ring_finish(
        a_1, y, bufs[0], ay_1, y_part.at[pl.ds(0, 3), row_cut[0]], y_part.at[pl.ds(0, 3), row_cut[1]]
    )
    ax_1 = ring_start(c_1, x, bufs[3], sems[3], at_x, (0, 1, 2, 3))

    hold_x[...] = small_sum(sy, small_y, y, small[y], NY)
    sx = small_start(3, lambda peer: hold_x, small_x, x, NX, at_x)

    ring_finish(bx_view, x, bufs[2], bx, x_part.at[pl.ds(0, 2)], x_part.at[pl.ds(2, 2)])
    by = ring_start(by_view, y, bufs[4], sems[4], at_y, (0, 1, 2, 3))
    ax_1 = ring_middle(c_1, x, bufs[3], sems[3], at_x, ax_1)
    ring_finish(
        a_2, y, bufs[1], ay_2, y_part.at[pl.ds(3, 2), row_cut[0]], y_part.at[pl.ds(3, 2), row_cut[1]]
    )
    ax_2 = ring_start(c_2, x, bufs[5], sems[5], at_x, (0, 1, 2, 3))

    hold_z[...] = small_sum(sx, small_x, x, hold_x[...], NX)
    sz = small_start(6, lambda peer: hold_z, small_z, z, NZ, at_z)

    by = ring_middle(by_view, y, bufs[4], sems[4], at_y, by)
    ax_2 = ring_middle(c_2, x, bufs[5], sems[5], at_x, ax_2)
    ring_finish(c_1, x, bufs[3], ax_1, total.at[pl.ds(0, 2)], total.at[pl.ds(2, 1)])
    send_last((0, 1, 2))
    ring_finish(by_view, y, bufs[4], by, total.at[pl.ds(ZA, 2)], total.at[pl.ds(ZA + 2, 1)])
    send_last((5, 6, 7))
    ring_finish(c_2, x, bufs[5], ax_2, total.at[pl.ds(3, 1)], total.at[pl.ds(4, 1)])
    send_last((3, 4))

    out_small[...] = small_sum(sz, small_z, z, hold_z[...], NZ)
    value = total[z]
    for k in (1, 7, 2, 6, 3, 5, 4):
        peer = (z + k) % NZ
        last_copy(peer, peer).wait_recv()
        value = value + arrived[peer]
    out[...] = value
    sent = [right_head, left_tail, right_tail, left_head, relay_right, relay_left]
    for copies in (sent, swaps, mates, sy, sx, sz, ay_1, ay_2, bx, ax_1, by, ax_2):
        for copy in copies:
            copy.wait_send()
    for k in range(1, NZ):
        last_copy((z + k) % NZ, z).wait_send()


def finish_kernel(block, sums, owned, right, blocks):
    z, x, y, c = place()
    skip = x * 30 - jnp.minimum(x * 30 // 8, 10) * 8
    cross_factor = SATS / math.sqrt(512 * EPOCHS)
    factor = SATS / (512 * SLOTS * EPOCHS)
    value = pltpu.roll(block[...], COVER - skip, 0)[0:30, 0:ROWS]
    row = (z * NX + x) * 30 + lax.broadcasted_iota(jnp.int32, (30, ROWS), 0)
    column = (y * 2 + c) * ROWS + lax.broadcasted_iota(jnp.int32, (30, ROWS), 1)
    owned[...] = jnp.where(row // PAR == column // PAR, 0.0, value) * cross_factor
    right[...] = sums[8:9, 0:ROWS] * factor
    scaled = jnp.broadcast_to((sums[0:8] * factor)[:, None, :], (PAR, PAR, 128))
    place_of = lax.broadcasted_iota(jnp.int32, (PAR, PAR, 128), 2) % PAR
    inner = lax.broadcasted_iota(jnp.int32, (PAR, PAR, 128), 1)
    rows = jnp.where(place_of == inner, scaled, 0.0).reshape(PAR * PAR, 128)
    to = lax.broadcasted_iota(jnp.int32, (128, 128), 0)
    lane = lax.broadcasted_iota(jnp.int32, (128, 128), 1)
    moved = turned(rows, jnp.where(to == lane // PAR, 1.0, 0.0), HIGH)
    blocks[...] = moved.reshape(PAR, PAR, 128)[:, :, 0:OWN]


def ring_buffers(half_0, half_1):
    shapes = [half_0, half_1, half_0, half_1, half_0, half_1, half_0, half_1]
    return [pltpu.VMEM(shape, F32) for shape in shapes]


def shards(sight, mapping, residual, counts, track, knots, orbit):
    shape = jax.ShapeDtypeStruct
    stations = (sight, mapping, residual, counts, knots)
    nb = NZ - ZA
    big = 4 * EPOCHS
    scratch = (
        [pltpu.VMEM(a.shape, a.dtype) for a in stations] * 2
        + [
            pltpu.SMEM((2, SLOTS), jnp.int32),
            pltpu.VMEM((2, 128), jnp.int32),
            pltpu.VMEM((2, 128), jnp.int32),
            pltpu.SMEM((2, 128), jnp.int32),
            pltpu.SMEM((2, 128), jnp.int32),
            pltpu.VMEM((SATS, 3, PAR, EPOCHS), F32),
            pltpu.VMEM((4, 3, SLOTS + 8, EPOCHS), F32),
            pltpu.VMEM((4, 3, SLOTS + 8, EPOCHS), F32),
            pltpu.VMEM((1024, big), BF16),
            pltpu.VMEM((1024, big), BF16),
            pltpu.VMEM((128, big), BF16),
            pltpu.VMEM((128, big), BF16),
            pltpu.VMEM((128, 2 * big), BF16),
            pltpu.VMEM((128, 2 * big), BF16),
            pltpu.VMEM((128, 2 * big), BF16),
            pltpu.VMEM((1024, 128), BF16),
            pltpu.VMEM((1024, 128), BF16),
            pltpu.VMEM((NY, NZ, 128, 128), F32),
            pltpu.VMEM((NY, PAR, 128), F32),
            pltpu.VMEM((NY, 16, 128), F32),
        ]
        + ring_buffers((3, 64, 128), (3, ROWS - 64, 128))
        + ring_buffers((2, 64, 128), (2, ROWS - 64, 128))
        + ring_buffers((2, nb, COVER, 128), (2, nb, COVER, 128))
        + ring_buffers((2, COVER, 128), (1, COVER, 128))
        + ring_buffers((2, COVER, 128), (1, COVER, 128))
        + ring_buffers((1, COVER, 128), (1, COVER, 128))
        + [
            pltpu.VMEM((ZA, ROWS, 128), F32),
            pltpu.VMEM((NY, nb, COVER, 128), F32),
            pltpu.VMEM((NZ, COVER, 128), F32),
            pltpu.VMEM((NZ, COVER, 128), F32),
            pltpu.VMEM((NY, 16, 128), F32),
            pltpu.VMEM((NX, 16, 128), F32),
            pltpu.VMEM((NZ, 16, 128), F32),
            pltpu.VMEM((16, 128), F32),
            pltpu.VMEM((16, 128), F32),
            pltpu.SemaphoreType.DMA((19,)),
            pltpu.SemaphoreType.DMA((19,)),
            pltpu.SemaphoreType.DMA((9,)),
        ]
        + [pltpu.SemaphoreType.DMA((6,))] * 12
        + [
            pltpu.SemaphoreType.DMA((NZ,)),
            pltpu.SemaphoreType.DMA((NZ,)),
            pltpu.SemaphoreType.DMA((13,)),
            pltpu.SemaphoreType.DMA((13,)),
        ]
    )
    block, sums = pl.pallas_call(
        main_kernel,
        name="network",
        out_shape=[shape((COVER, 128), F32), shape((16, 128), F32)],
        in_specs=[ANY] * 7,
        out_specs=[VMEM, VMEM],
        scratch_shapes=scratch,
        compiler_params=pltpu.CompilerParams(
            collective_id=0, has_side_effects=True, vmem_limit_bytes=60 * 1024 * 1024
        ),
    )(track, orbit, *stations)

    owned, right, blocks = pl.pallas_call(
        finish_kernel,
        name="finish",
        out_shape=[
            shape((30, ROWS), F32),
            shape((1, ROWS), F32),
            shape((PAR, PAR, OWN), F32),
        ],
        in_specs=[VMEM, VMEM],
        out_specs=[VMEM] * 3,
    )(block, sums)
    return owned.T, right.reshape(ROWS), jnp.transpose(blocks, (2, 0, 1))


def solution(mesh):
    placed = (
        P(("sta", "sat"), None, None, None),
        P(("sta", "sat"), None, None),
        P(("sta", "sat"), None, None),
        P(("sta", "sat"), None, None),
        P(("sta", "sat"), None),
        P(("sta", "sat"), None),
        P("sat", None, None, None),
    )
    return jax.shard_map(
        shards,
        mesh=mesh,
        in_specs=placed,
        out_specs=(P("sat", "sta"), P("sat"), P("sat", None, None)),
        check_vma=False,
    )
```

```python
import functools
import math

import jax
import jax.numpy as jnp
from jax import lax
from jax.experimental import pallas as pl
from jax.experimental.pallas import tpu as pltpu
from jax.sharding import PartitionSpec as P

F32 = jnp.float32
BF16 = jnp.bfloat16
MESH = pl.DeviceIdType.MESH
HIGH = lax.Precision.HIGHEST

SATS = 120
OWN = 15
PAR = 8
SLOTS = 32
EPOCHS = 256
KNOTS = 4
PRIOR = 1.0
NY = 4
NX = 4
NZ = 8
ROWS = 120
COVER = 32
CUT = 8
ZA = 5
ANY = pl.BlockSpec(memory_space=pl.ANY)
VMEM = pl.BlockSpec(memory_space=pltpu.VMEM)
SMEM = pl.BlockSpec(memory_space=pltpu.SMEM)


def place():
    sta = lax.axis_index("sta")
    sat = lax.axis_index("sat")
    return sta // NX, sta % NX, sat // 2, sat % 2


def remote(src, dst, send, recv, device):
    return pltpu.make_async_remote_copy(
        src_ref=src,
        dst_ref=dst,
        send_sem=send,
        recv_sem=recv,
        device_id=device,
        device_id_type=MESH,
    )


def greet(peers):
    barrier = pltpu.get_barrier_semaphore()
    for peer in peers:
        pl.semaphore_signal(barrier, inc=1, device_id=peer, device_id_type=MESH)
    pl.semaphore_wait(barrier, len(peers))


def halves(value):
    high = value.astype(BF16)
    low = (value - high.astype(F32)).astype(BF16)
    return high, low


def turned(a, b, precision=None):
    return lax.dot_general(
        a, b, (((1,), (1,)), ((), ())), preferred_element_type=F32, precision=precision
    )


def product(a_high, a_low, b_high, b_low):
    return turned(a_high, b_high) + turned(a_high, b_low) + turned(a_low, b_high)


def ring_start(view, me, buffers, sems, device, slots):
    far, right, left = (me + 2) % 4, (me + 1) % 4, (me + 3) % 4
    b_0, b_1, l_0, l_1, r_0, r_1 = buffers[:6]
    send, recv = sems
    plan = (
        (view(far, 0), b_0, right),
        (view(far, 1), b_1, left),
        (view(right, 1), l_1, right),
        (view(left, 0), r_0, left),
    )
    copies = []
    for slot in slots:
        src, dst, peer = plan[slot]
        copy = remote(src, dst, send.at[slot], recv.at[slot], device(peer))
        copy.start()
        copies.append(copy)
    return copies


def ring_middle(view, me, buffers, sems, device, copies):
    right, left = (me + 1) % 4, (me + 3) % 4
    b_0, b_1, l_0, l_1, r_0, r_1, s_0, s_1 = buffers
    send, recv = sems
    copies[0].wait_recv()
    s_0[...] = view(right, 0)[...] + b_0[...]
    one = remote(s_0, l_0, send.at[4], recv.at[4], device(right))
    one.start()
    copies[1].wait_recv()
    s_1[...] = view(left, 1)[...] + b_1[...]
    two = remote(s_1, r_1, send.at[5], recv.at[5], device(left))
    two.start()
    return copies + [one, two]


def ring_finish(view, me, buffers, copies, out_0, out_1):
    b_0, b_1, l_0, l_1, r_0, r_1 = buffers[:6]
    for index in (2, 3, 4, 5):
        copies[index].wait_recv()
    out_0[...] = view(me, 0)[...] + l_0[...] + r_0[...]
    out_1[...] = view(me, 1)[...] + l_1[...] + r_1[...]


def main_kernel(*refs):
    track, orbit = refs[0:2]
    given = refs[2:7]
    out, out_small = refs[7:9]
    refs = refs[9:]
    mine, other, refs = refs[:5], refs[5:10], refs[10:]
    (track_s, ids_v, ids_w, ids_a, ids_b, full, sv, factors, f_high, f_low, u_high, u_low,
     t_high, t_low, pick, e_left, e_right, normal, own_sum, small), refs = refs[:20], refs[20:]
    bufs, refs = [refs[i * 8 : (i + 1) * 8] for i in range(6)], refs[48:]
    (y_part, x_part, total, arrived, small_y, small_x, small_z, hold_x, hold_z), refs = (
        refs[:9], refs[9:])
    g_send, g_recv, local = refs[:3]
    refs = refs[3:]
    sems = [(refs[2 * i], refs[2 * i + 1]) for i in range(6)]
    z_send, z_recv, s_send, s_recv = refs[12:]
    z, x, y, c = place()

    def at_y(peer):
        return (z * NX + x, peer * 2 + c)

    def at_x(peer):
        return (z * NX + peer, y * 2 + c)

    def at_z(peer):
        return (peer * NX + x, y * 2 + c)

    mate = (z * NX + x, y * 2 + 1 - c)
    far, right, left = (y + 2) % NY, (y + 1) % NY, (y + 3) % NY
    head, tail = (0, CUT), (CUT, OWN - CUT)

    def base_of(chip, core):
        return (chip * 2 + core) * OWN

    def part(chip, cut):
        return full.at[pl.ds(base_of(chip, c) + cut[0], cut[1])]

    def own(cut):
        return orbit.at[pl.ds(cut[0], cut[1])]

    keeps = [
        pltpu.make_async_copy(a, b, local.at[i])
        for i, (a, b) in enumerate(
            zip(
                (track,) + given + (orbit,),
                (track_s,) + mine + (full.at[pl.ds(base_of(y, c), OWN)],),
            )
        )
    ]
    for copy in keeps:
        copy.start()

    greet(
        [at_y((y + k) % NY) for k in range(1, NY)]
        + [at_x((x + k) % NX) for k in range(1, NX)]
        + [at_z((z + k) % NZ) for k in range(1, NZ)]
        + [mate]
    )

    def go(slot, src, dst, device):
        copy = remote(src, dst, g_send.at[slot], g_recv.at[slot], device)
        copy.start()
        return copy

    right_head = go(0, own(head), part(y, head), at_y(right))
    left_tail = go(1, own(tail), part(y, tail), at_y(left))
    right_tail = go(2, own(tail), part(y, tail), at_y(right))
    left_head = go(3, own(head), part(y, head), at_y(left))
    swaps = [go(7 + i, a, b, mate) for i, (a, b) in enumerate(zip(given, other))]
    mate_own = go(12, orbit, full.at[pl.ds(base_of(y, c), OWN)], mate)

    keeps[0].wait()
    place_lane = lax.broadcasted_iota(jnp.int32, (1, 128), 1)
    for s in range(2):
        slots = jnp.full((1, 128), SLOTS, jnp.int32)
        for m in range(SLOTS):
            slots = jnp.where(place_lane == track_s[s, m], m, slots)
        ids_v[s : s + 1, :] = slots
    hand_a = pltpu.make_async_copy(ids_v, ids_a, local.at[7])
    hand_a.start()
    swaps.append(go(6, ids_v, ids_w, mate))

    blank = jnp.zeros((4, 3, 8, EPOCHS), F32)
    sv[:, :, SLOTS:, :] = blank
    factors[:, :, SLOTS:, :] = blank
    lane_rows = lax.broadcasted_iota(jnp.int32, (128, EPOCHS), 0)
    row8 = lax.broadcasted_iota(jnp.int32, (8, EPOCHS), 0)
    pick_last = jnp.where((lane_rows % 32 == 16) & (lane_rows < 96), 1.0, 0.0).astype(BF16)

    pick[:, 4 * EPOCHS :] = pick_last

    def prepare(index):
        sight, mapping, residual, counts, knots = mine if index < 2 else other
        s = index % 2
        chosen = lane_rows % 32 == knots[s : s + 1, :] + KNOTS * index
        chosen = jnp.where(chosen & (lane_rows < 96), 1.0, 0.0)
        wide = EPOCHS * index
        pick[:, wide : wide + EPOCHS] = chosen.astype(BF16)
        weight = counts[s].astype(F32)
        path = mapping[s]
        seen = residual[s]
        shared = jnp.maximum(jnp.sum(weight, 0, keepdims=True), 1.0)
        share = 1.0 / shared
        root = lax.rsqrt(shared)
        grow = shared * root
        weight_map = weight * path
        sum_map = jnp.sum(weight_map, 0, keepdims=True)
        sum_res = jnp.sum(weight * seen, 0, keepdims=True)
        scaled = weight * root
        for k in range(3):
            sv[index, k, 0:SLOTS] = sight[s, k] * scaled
        factors[index, 0, 0:SLOTS] = jnp.where(
            weight > 0.0, lax.rsqrt(jnp.maximum(weight, 1.0)) * grow, 0.0
        )
        factors[index, 1, 0:SLOTS] = (path - sum_map * share) * grow
        factors[index, 2, 0:SLOTS] = (seen - sum_res * share) * grow
        square = jnp.sum(weight_map * path, 0, keepdims=True) - sum_map * sum_map * share
        cross = jnp.sum(weight_map * seen, 0, keepdims=True) - sum_map * sum_res * share
        pair = jnp.where(row8 == 0, square, jnp.where(row8 == 1, cross, 0.0))
        return turned(pair, chosen, HIGH)

    own_row = lax.broadcasted_iota(jnp.int32, (128, 128), 0) // PAR
    own_lane = lax.broadcasted_iota(jnp.int32, (128, 128), 1) // PAR
    lane = lax.broadcasted_iota(jnp.int32, (1, 128), 1)

    def squeeze(block):
        block = jnp.where(own_row == own_lane, block, 0.0)
        return jnp.sum(block.reshape(16, PAR, 128), 0)

    def build(chip, core, sides, diagonal):
        base = base_of(chip, core)
        group = chip * 2 + core
        top = group * 128

        def one(j, index):
            ids = ids_a if index < 2 else ids_b
            slot = ids[index % 2, base + j]
            value = (
                sv[index, 0, pl.ds(slot, 1), :] * full[base + j, 0]
                + sv[index, 1, pl.ds(slot, 1), :] * full[base + j, 1]
                + sv[index, 2, pl.ds(slot, 1), :] * full[base + j, 2]
            )
            times = [
                value * factors[index, k, pl.ds(slot, 1), :]
                for k in range(3)
                if (diagonal if k == 0 else sides)
            ]
            return [value] + times

        def fill(k, second):
            row = pl.multiple_of(top + k * 16, 16)
            inner = pl.multiple_of(k * 16, 16)

            def put(high_ref, low_ref, rows, lanes, value):
                high_ref[pl.ds(rows, 16), lanes], low_ref[pl.ds(rows, 16), lanes] = halves(value)

            gathered = 0.0
            for index in range(4):
                lanes = slice(index * EPOCHS, (index + 1) * EPOCHS)
                a = one(2 * k, index)
                b = one(2 * k + 1, index) if second else [jnp.zeros_like(i) for i in a]
                values = [jnp.concatenate([i, j], axis=0) for i, j in zip(a, b)]
                if diagonal:
                    put(u_high, u_low, inner, lanes, values[1])
                if sides:
                    put(f_high, f_low, row, lanes, values[0])
                    put(t_high, t_low, inner, lanes, values[-2])
                    gathered = gathered + values[-1]
            if sides:
                put(t_high, t_low, inner, slice(4 * EPOCHS, 5 * EPOCHS), gathered)

        def step(k, carry):
            fill(k, True)
            return carry

        lax.fori_loop(0, 7, step, 0)
        fill(7, False)
        if sides:
            side = turned(t_high[...], pick[...]) + turned(t_low[...], pick[...])
            rows = pl.ds(pl.multiple_of(top, 128), 128)
            high, low = halves(side * scale)
            high, low = high.astype(F32), low.astype(F32)
            e_left[rows] = jnp.where(lane < 64, high, low).astype(BF16)
            high, low = halves(side * right_scale)
            high, low = high.astype(F32), low.astype(F32)
            e_right[rows] = jnp.where((lane >= 32) & (lane < 64), low, high).astype(BF16)
        if diagonal:
            rows = pl.ds(pl.multiple_of(top, 128), 128)
            v_high, v_low = f_high[rows], f_low[rows]
            own_sum[chip] = squeeze(
                product(u_high[...], u_low[...], u_high[...], u_low[...])
                - product(v_high, v_low, v_high, v_low)
                - turned(e_left[rows], e_right[rows])
            )

    for copy in keeps[1:]:
        copy.wait()
    hand_a.wait()
    local_rows = prepare(0) + prepare(1)
    for copy in swaps:
        copy.wait_recv()
    hand_b = pltpu.make_async_copy(ids_w, ids_b, local.at[8])
    hand_b.start()
    local_rows = local_rows + prepare(2) + prepare(3)
    scale = jnp.where(lane % 32 < 16, lax.rsqrt(local_rows[0:1] + PRIOR), 0.0)
    right_scale = jnp.where(lane % 32 < 16, scale, 1.0)
    special = jnp.where(lane % 32 == 16, -1.0, local_rows[1:2] * scale)
    hand_b.wait()
    build(y, c, True, True)
    mates = [mate_own]
    right_head.wait_recv()
    relay_right = go(4, part(left, head), part(left, head), at_y(right))
    mates.append(go(13, part(left, head), part(left, head), mate))
    left_tail.wait_recv()
    relay_left = go(5, part(right, tail), part(right, tail), at_y(left))
    mates.append(go(14, part(right, tail), part(right, tail), mate))
    mate_own.wait_recv()
    build(y, 1 - c, True, False)
    right_tail.wait_recv()
    mates.append(go(15, part(left, tail), part(left, tail), mate))
    left_head.wait_recv()
    mates.append(go(16, part(right, head), part(right, head), mate))
    build(left, c, True, True)
    build(right, c, True, True)
    for copy in mates[1:]:
        copy.wait_recv()
    build(left, 1 - c, True, False)
    build(right, 1 - c, True, False)
    relay_right.wait_recv()
    mates.append(go(17, part(far, head), part(far, head), mate))
    relay_left.wait_recv()
    mates.append(go(18, part(far, tail), part(far, tail), mate))
    build(far, c, True, False)
    for copy in mates[5:]:
        copy.wait_recv()
    build(far, 1 - c, True, False)

    row = lax.broadcasted_iota(jnp.int32, (8, 128), 0)
    high, low = halves(jnp.where(row == 0, special, 0.0))
    special = jnp.where(lane < 64, high.astype(F32), low.astype(F32))
    e_left[112:128] = jnp.concatenate(
        [e_left[112:128].astype(F32)[0:8], special], axis=0
    ).astype(BF16)

    def multiply(first, count, slabs):
        rows = slice(first * 128, (first + count) * 128)
        own_rows = [pl.ds(pl.multiple_of((slab * 2 + c) * 128, 128), 128) for slab in slabs]
        r_high, r_low, r_side = [
            jnp.concatenate([ref[i] for i in own_rows], axis=0)
            for ref in (f_high, f_low, e_right)
        ]
        result = product(f_high[rows], f_low[rows], r_high, r_low) + turned(e_left[rows], r_side)
        for i, slab in enumerate(slabs):
            lanes = slice(i * 128, (i + 1) * 128)
            for group in range(count):
                for q in range(NX):
                    at = group * 128 + q * 30
                    normal[slab, first + group, q * COVER : (q + 1) * COVER] = -result[
                        at : at + COVER, lanes
                    ]

    def rows_of(peer):
        return pl.ds(pl.multiple_of(peer * COVER, COVER), COVER)

    row_cut = (pl.ds(0, 64), pl.ds(64, 64))
    cuts = ((pl.ds(0, 2), pl.ds(2, 1)), (pl.ds(3, 1), pl.ds(4, 1)))
    b_cut = (pl.ds(0, 2), pl.ds(2, 1))

    def first_view(which):
        zs = (pl.ds(0, 3), pl.ds(3, 2))[which]
        return lambda peer, half: normal.at[peer, zs, row_cut[half]]

    def second_view(which):
        return lambda peer, half: y_part.at[cuts[which][half], rows_of(peer)]

    def bx_view(peer, half):
        return normal.at[pl.ds(2 * half, 2), pl.ds(ZA, NZ - ZA), rows_of(peer)]

    def by_view(peer, half):
        return x_part.at[peer, b_cut[half]]

    def small_start(base, source, target, me, size, device):
        copies = []
        for k in range(1, size):
            peer = (me + k) % size
            slot = base + k - 1
            copy = remote(
                source(peer), target.at[me], s_send.at[slot], s_recv.at[slot], device(peer)
            )
            copy.start()
            copies.append(copy)
        return copies

    def small_sum(copies, target, me, own, size):
        target[me] = own
        for copy in copies:
            copy.wait_recv()
        result = target[0]
        for k in range(1, size):
            result = result + target[k]
        return result

    def last_copy(peer, slot):
        return remote(
            total.at[peer], arrived.at[slot], z_send.at[peer], z_recv.at[slot], at_z(peer)
        )

    def send_last(peers):
        for peer in peers:
            @pl.when(z != peer)
            def _():
                last_copy(peer, z).start()

    a_1, a_2 = first_view(0), first_view(1)
    multiply(0, 3, (far, right))
    ay_1 = ring_start(a_1, y, bufs[0], sems[0], at_y, (0, 1, 2))
    multiply(ZA, NZ - ZA, (far, right))
    multiply(ZA, NZ - ZA, (left, y))
    bx = ring_start(bx_view, x, bufs[2], sems[2], at_x, (0, 1, 2, 3))
    multiply(3, 2, (far, right))
    ay_2 = ring_start(a_2, y, bufs[1], sems[1], at_y, (0, 1, 2))
    multiply(0, 3, (left, y))
    ay_1 += ring_start(a_1, y, bufs[0], sems[0], at_y, (3,))
    multiply(3, 2, (left, y))
    ay_2 += ring_start(a_2, y, bufs[1], sems[1], at_y, (3,))
    ay_1 = ring_middle(a_1, y, bufs[0], sems[0], at_y, ay_1)

    build(far, c, False, True)
    for slab in range(NY):
        small[slab, 0:8] = own_sum[slab]
        small[slab, 8:16] = normal[slab, 0, ROWS : ROWS + 8, :]
    sy = small_start(0, lambda peer: small.at[peer], small_y, y, NY, at_y)

    bx = ring_middle(bx_view, x, bufs[2], sems[2], at_x, bx)
    ay_2 = ring_middle(a_2, y, bufs[1], sems[1], at_y, ay_2)

    c_1, c_2 = second_view(0), second_view(1)
    ring_finish(
        a_1, y, bufs[0], ay_1, y_part.at[pl.ds(0, 3), row_cut[0]], y_part.at[pl.ds(0, 3), row_cut[1]]
    )
    ax_1 = ring_start(c_1, x, bufs[3], sems[3], at_x, (0, 1, 2, 3))

    hold_x[...] = small_sum(sy, small_y, y, small[y], NY)
    sx = small_start(3, lambda peer: hold_x, small_x, x, NX, at_x)

    ring_finish(bx_view, x, bufs[2], bx, x_part.at[pl.ds(0, 2)], x_part.at[pl.ds(2, 2)])
    by = ring_start(by_view, y, bufs[4], sems[4], at_y, (0, 1, 2, 3))
    ax_1 = ring_middle(c_1, x, bufs[3], sems[3], at_x, ax_1)
    ring_finish(
        a_2, y, bufs[1], ay_2, y_part.at[pl.ds(3, 2), row_cut[0]], y_part.at[pl.ds(3, 2), row_cut[1]]
    )
    ax_2 = ring_start(c_2, x, bufs[5], sems[5], at_x, (0, 1, 2, 3))

    hold_z[...] = small_sum(sx, small_x, x, hold_x[...], NX)
    sz = small_start(6, lambda peer: hold_z, small_z, z, NZ, at_z)

    by = ring_middle(by_view, y, bufs[4], sems[4], at_y, by)
    ax_2 = ring_middle(c_2, x, bufs[5], sems[5], at_x, ax_2)
    ring_finish(c_1, x, bufs[3], ax_1, total.at[pl.ds(0, 2)], total.at[pl.ds(2, 1)])
    send_last((0, 1, 2))
    ring_finish(by_view, y, bufs[4], by, total.at[pl.ds(ZA, 2)], total.at[pl.ds(ZA + 2, 1)])
    send_last((5, 6, 7))
    ring_finish(c_2, x, bufs[5], ax_2, total.at[pl.ds(3, 1)], total.at[pl.ds(4, 1)])
    send_last((3, 4))

    out_small[...] = small_sum(sz, small_z, z, hold_z[...], NZ)
    value = total[z]
    for k in (1, 7, 2, 6, 3, 5, 4):
        peer = (z + k) % NZ
        last_copy(peer, peer).wait_recv()
        value = value + arrived[peer]
    out[...] = value
    sent = [right_head, left_tail, right_tail, left_head, relay_right, relay_left]
    for copies in (sent, swaps, mates, sy, sx, sz, ay_1, ay_2, bx, ax_1, by, ax_2):
        for copy in copies:
            copy.wait_send()
    for k in range(1, NZ):
        last_copy((z + k) % NZ, z).wait_send()


def finish_kernel(block, sums, owned, right, blocks):
    z, x, y, c = place()
    cross_factor = SATS / math.sqrt(512 * EPOCHS)
    factor = SATS / (512 * SLOTS * EPOCHS)
    value = block[0:30, 0:ROWS]
    row = (z * NX + x) * 30 + lax.broadcasted_iota(jnp.int32, (30, ROWS), 0)
    column = (y * 2 + c) * ROWS + lax.broadcasted_iota(jnp.int32, (30, ROWS), 1)
    owned[...] = jnp.where(row // PAR == column // PAR, 0.0, value) * cross_factor
    right[...] = sums[14:15, 0:ROWS] * factor
    scaled = jnp.broadcast_to((sums[0:8] * factor)[:, None, :], (PAR, PAR, 128))
    place_of = lax.broadcasted_iota(jnp.int32, (PAR, PAR, 128), 2) % PAR
    inner = lax.broadcasted_iota(jnp.int32, (PAR, PAR, 128), 1)
    rows = jnp.where(place_of == inner, scaled, 0.0).reshape(PAR * PAR, 128)
    to = lax.broadcasted_iota(jnp.int32, (128, 128), 0)
    lane = lax.broadcasted_iota(jnp.int32, (128, 128), 1)
    moved = turned(rows, jnp.where(to == lane // PAR, 1.0, 0.0), HIGH)
    blocks[...] = moved.reshape(PAR, PAR, 128)[:, :, 0:OWN]


def ring_buffers(half_0, half_1):
    shapes = [half_0, half_1, half_0, half_1, half_0, half_1, half_0, half_1]
    return [pltpu.VMEM(shape, F32) for shape in shapes]


def shards(sight, mapping, residual, counts, track, knots, orbit):
    shape = jax.ShapeDtypeStruct
    stations = (sight, mapping, residual, counts, knots)
    nb = NZ - ZA
    big = 4 * EPOCHS
    scratch = (
        [pltpu.VMEM(a.shape, a.dtype) for a in stations] * 2
        + [
            pltpu.SMEM((2, SLOTS), jnp.int32),
            pltpu.VMEM((2, 128), jnp.int32),
            pltpu.VMEM((2, 128), jnp.int32),
            pltpu.SMEM((2, 128), jnp.int32),
            pltpu.SMEM((2, 128), jnp.int32),
            pltpu.VMEM((SATS, 3, PAR, EPOCHS), F32),
            pltpu.VMEM((4, 3, SLOTS + 8, EPOCHS), F32),
            pltpu.VMEM((4, 3, SLOTS + 8, EPOCHS), F32),
            pltpu.VMEM((1024, big), BF16),
            pltpu.VMEM((1024, big), BF16),
            pltpu.VMEM((128, big), BF16),
            pltpu.VMEM((128, big), BF16),
            pltpu.VMEM((128, big + EPOCHS), BF16),
            pltpu.VMEM((128, big + EPOCHS), BF16),
            pltpu.VMEM((128, big + EPOCHS), BF16),
            pltpu.VMEM((1024, 128), BF16),
            pltpu.VMEM((1024, 128), BF16),
            pltpu.VMEM((NY, NZ, 128, 128), F32),
            pltpu.VMEM((NY, PAR, 128), F32),
            pltpu.VMEM((NY, 16, 128), F32),
        ]
        + ring_buffers((3, 64, 128), (3, 64, 128))
        + ring_buffers((2, 64, 128), (2, 64, 128))
        + ring_buffers((2, nb, COVER, 128), (2, nb, COVER, 128))
        + ring_buffers((2, COVER, 128), (1, COVER, 128))
        + ring_buffers((2, COVER, 128), (1, COVER, 128))
        + ring_buffers((1, COVER, 128), (1, COVER, 128))
        + [
            pltpu.VMEM((ZA, 128, 128), F32),
            pltpu.VMEM((NY, nb, COVER, 128), F32),
            pltpu.VMEM((NZ, COVER, 128), F32),
            pltpu.VMEM((NZ, COVER, 128), F32),
            pltpu.VMEM((NY, 16, 128), F32),
            pltpu.VMEM((NX, 16, 128), F32),
            pltpu.VMEM((NZ, 16, 128), F32),
            pltpu.VMEM((16, 128), F32),
            pltpu.VMEM((16, 128), F32),
            pltpu.SemaphoreType.DMA((19,)),
            pltpu.SemaphoreType.DMA((19,)),
            pltpu.SemaphoreType.DMA((9,)),
        ]
        + [pltpu.SemaphoreType.DMA((6,))] * 12
        + [
            pltpu.SemaphoreType.DMA((NZ,)),
            pltpu.SemaphoreType.DMA((NZ,)),
            pltpu.SemaphoreType.DMA((13,)),
            pltpu.SemaphoreType.DMA((13,)),
        ]
    )
    block, sums = pl.pallas_call(
        main_kernel,
        name="network",
        out_shape=[shape((COVER, 128), F32), shape((16, 128), F32)],
        in_specs=[ANY] * 7,
        out_specs=[VMEM, VMEM],
        scratch_shapes=scratch,
        compiler_params=pltpu.CompilerParams(
            collective_id=0, has_side_effects=True, vmem_limit_bytes=60 * 1024 * 1024
        ),
    )(track, orbit, *stations)

    owned, right, blocks = pl.pallas_call(
        finish_kernel,
        name="finish",
        out_shape=[
            shape((30, ROWS), F32),
            shape((1, ROWS), F32),
            shape((PAR, PAR, OWN), F32),
        ],
        in_specs=[VMEM, VMEM],
        out_specs=[VMEM] * 3,
    )(block, sums)
    return owned.T, right.reshape(ROWS), jnp.transpose(blocks, (2, 0, 1))


def solution(mesh):
    placed = (
        P(("sta", "sat"), None, None, None),
        P(("sta", "sat"), None, None),
        P(("sta", "sat"), None, None),
        P(("sta", "sat"), None, None),
        P(("sta", "sat"), None),
        P(("sta", "sat"), None),
        P("sat", None, None, None),
    )
    return jax.shard_map(
        shards,
        mesh=mesh,
        in_specs=placed,
        out_specs=(P("sat", "sta"), P("sat"), P("sat", None, None)),
        check_vma=False,
    )
```

```python
import functools
import math

import jax
import jax.numpy as jnp
from jax import lax
from jax.experimental import pallas as pl
from jax.experimental.pallas import tpu as pltpu
from jax.sharding import PartitionSpec as P

F32 = jnp.float32
BF16 = jnp.bfloat16
MESH = pl.DeviceIdType.MESH
HIGH = lax.Precision.HIGHEST

SATS = 120
OWN = 15
PAR = 8
SLOTS = 32
EPOCHS = 256
KNOTS = 4
PRIOR = 1.0
NY = 4
NX = 4
NZ = 8
ROWS = 120
COVER = 32
CUT = 8
ZA = 4
ANY = pl.BlockSpec(memory_space=pl.ANY)
VMEM = pl.BlockSpec(memory_space=pltpu.VMEM)
SMEM = pl.BlockSpec(memory_space=pltpu.SMEM)


def place():
    sta = lax.axis_index("sta")
    sat = lax.axis_index("sat")
    return sta // NX, sta % NX, sat // 2, sat % 2


def remote(src, dst, send, recv, device):
    return pltpu.make_async_remote_copy(
        src_ref=src,
        dst_ref=dst,
        send_sem=send,
        recv_sem=recv,
        device_id=device,
        device_id_type=MESH,
    )


def greet(peers):
    barrier = pltpu.get_barrier_semaphore()
    for peer in peers:
        pl.semaphore_signal(barrier, inc=1, device_id=peer, device_id_type=MESH)
    pl.semaphore_wait(barrier, len(peers))


def halves(value):
    high = value.astype(BF16)
    low = (value - high.astype(F32)).astype(BF16)
    return high, low


def turned(a, b, precision=None):
    return lax.dot_general(
        a, b, (((1,), (1,)), ((), ())), preferred_element_type=F32, precision=precision
    )


def product(a_high, a_low, b_high, b_low):
    return turned(a_high, b_high) + turned(a_high, b_low) + turned(a_low, b_high)


def ring_start(view, me, buffers, sems, device, slots):
    far, right, left = (me + 2) % 4, (me + 1) % 4, (me + 3) % 4
    b_0, b_1, l_0, l_1, r_0, r_1 = buffers[:6]
    send, recv = sems
    plan = (
        (view(far, 0), b_0, right),
        (view(far, 1), b_1, left),
        (view(right, 1), l_1, right),
        (view(left, 0), r_0, left),
    )
    copies = []
    for slot in slots:
        src, dst, peer = plan[slot]
        copy = remote(src, dst, send.at[slot], recv.at[slot], device(peer))
        copy.start()
        copies.append(copy)
    return copies


def ring_middle(view, me, buffers, sems, device, copies):
    right, left = (me + 1) % 4, (me + 3) % 4
    b_0, b_1, l_0, l_1, r_0, r_1, s_0, s_1 = buffers
    send, recv = sems
    copies[0].wait_recv()
    s_0[...] = view(right, 0)[...] + b_0[...]
    one = remote(s_0, l_0, send.at[4], recv.at[4], device(right))
    one.start()
    copies[1].wait_recv()
    s_1[...] = view(left, 1)[...] + b_1[...]
    two = remote(s_1, r_1, send.at[5], recv.at[5], device(left))
    two.start()
    return copies + [one, two]


def ring_finish(view, me, buffers, copies, out_0, out_1):
    b_0, b_1, l_0, l_1, r_0, r_1 = buffers[:6]
    for index in (2, 3, 4, 5):
        copies[index].wait_recv()
    out_0[...] = view(me, 0)[...] + l_0[...] + r_0[...]
    out_1[...] = view(me, 1)[...] + l_1[...] + r_1[...]


def main_kernel(*refs):
    track, orbit = refs[0:2]
    given = refs[2:7]
    out, out_small = refs[7:9]
    refs = refs[9:]
    mine, other, refs = refs[:5], refs[5:10], refs[10:]
    (track_s, ids_v, ids_w, ids_a, ids_b, full, sv, factors, f_high, f_low, u_high, u_low,
     t_high, t_low, pick, e_left, e_right, normal, own_sum, small), refs = refs[:20], refs[20:]
    bufs, refs = [refs[i * 8 : (i + 1) * 8] for i in range(8)], refs[64:]
    (y_part, x_part, total, arrived, small_y, small_x, small_z, hold_x, hold_z), refs = (
        refs[:9], refs[9:])
    g_send, g_recv, local = refs[:3]
    refs = refs[3:]
    sems = [(refs[2 * i], refs[2 * i + 1]) for i in range(8)]
    z_send, z_recv, s_send, s_recv = refs[16:]
    z, x, y, c = place()

    def at_y(peer):
        return (z * NX + x, peer * 2 + c)

    def at_x(peer):
        return (z * NX + peer, y * 2 + c)

    def at_z(peer):
        return (peer * NX + x, y * 2 + c)

    mate = (z * NX + x, y * 2 + 1 - c)
    far, right, left = (y + 2) % NY, (y + 1) % NY, (y + 3) % NY
    head, tail = (0, CUT), (CUT, OWN - CUT)

    def base_of(chip, core):
        return (chip * 2 + core) * OWN

    def part(chip, cut):
        return full.at[pl.ds(base_of(chip, c) + cut[0], cut[1])]

    def own(cut):
        return orbit.at[pl.ds(cut[0], cut[1])]

    keeps = [
        pltpu.make_async_copy(a, b, local.at[i])
        for i, (a, b) in enumerate(
            zip(
                (track,) + given + (orbit,),
                (track_s,) + mine + (full.at[pl.ds(base_of(y, c), OWN)],),
            )
        )
    ]
    for copy in keeps:
        copy.start()

    greet(
        [at_y((y + k) % NY) for k in range(1, NY)]
        + [at_x((x + k) % NX) for k in range(1, NX)]
        + [at_z((z + k) % NZ) for k in range(1, NZ)]
        + [mate]
    )

    def go(slot, src, dst, device):
        copy = remote(src, dst, g_send.at[slot], g_recv.at[slot], device)
        copy.start()
        return copy

    right_head = go(0, own(head), part(y, head), at_y(right))
    left_tail = go(1, own(tail), part(y, tail), at_y(left))
    right_tail = go(2, own(tail), part(y, tail), at_y(right))
    left_head = go(3, own(head), part(y, head), at_y(left))
    swaps = [go(7 + i, a, b, mate) for i, (a, b) in enumerate(zip(given, other))]
    mate_own = go(12, orbit, full.at[pl.ds(base_of(y, c), OWN)], mate)

    keeps[0].wait()
    place_lane = lax.broadcasted_iota(jnp.int32, (1, 128), 1)
    for s in range(2):
        slots = jnp.full((1, 128), SLOTS, jnp.int32)
        for m in range(SLOTS):
            slots = jnp.where(place_lane == track_s[s, m], m, slots)
        ids_v[s : s + 1, :] = slots
    hand_a = pltpu.make_async_copy(ids_v, ids_a, local.at[7])
    hand_a.start()
    swaps.append(go(6, ids_v, ids_w, mate))

    blank = jnp.zeros((4, 3, 8, EPOCHS), F32)
    sv[:, :, SLOTS:, :] = blank
    factors[:, :, SLOTS:, :] = blank
    lane_rows = lax.broadcasted_iota(jnp.int32, (128, EPOCHS), 0)
    row8 = lax.broadcasted_iota(jnp.int32, (8, EPOCHS), 0)
    pick_last = jnp.where((lane_rows % 32 == 16) & (lane_rows < 96), 1.0, 0.0).astype(BF16)

    pick[:, 4 * EPOCHS :] = pick_last

    def prepare(index):
        sight, mapping, residual, counts, knots = mine if index < 2 else other
        s = index % 2
        chosen = lane_rows % 32 == knots[s : s + 1, :] + KNOTS * index
        chosen = jnp.where(chosen & (lane_rows < 96), 1.0, 0.0)
        wide = EPOCHS * index
        pick[:, wide : wide + EPOCHS] = chosen.astype(BF16)
        weight = counts[s].astype(F32)
        path = mapping[s]
        seen = residual[s]
        shared = jnp.maximum(jnp.sum(weight, 0, keepdims=True), 1.0)
        share = 1.0 / shared
        root = lax.rsqrt(shared)
        grow = shared * root
        weight_map = weight * path
        sum_map = jnp.sum(weight_map, 0, keepdims=True)
        sum_res = jnp.sum(weight * seen, 0, keepdims=True)
        scaled = weight * root
        for k in range(3):
            sv[index, k, 0:SLOTS] = sight[s, k] * scaled
        factors[index, 0, 0:SLOTS] = jnp.where(
            weight > 0.0, lax.rsqrt(jnp.maximum(weight, 1.0)) * grow, 0.0
        )
        factors[index, 1, 0:SLOTS] = (path - sum_map * share) * grow
        factors[index, 2, 0:SLOTS] = (seen - sum_res * share) * grow
        square = jnp.sum(weight_map * path, 0, keepdims=True) - sum_map * sum_map * share
        cross = jnp.sum(weight_map * seen, 0, keepdims=True) - sum_map * sum_res * share
        pair = jnp.where(row8 == 0, square, jnp.where(row8 == 1, cross, 0.0))
        return turned(pair, chosen, HIGH)

    own_row = lax.broadcasted_iota(jnp.int32, (128, 128), 0) // PAR
    own_lane = lax.broadcasted_iota(jnp.int32, (128, 128), 1) // PAR
    lane = lax.broadcasted_iota(jnp.int32, (1, 128), 1)

    def squeeze(block):
        block = jnp.where(own_row == own_lane, block, 0.0)
        return jnp.sum(block.reshape(16, PAR, 128), 0)

    def build(chip, core, sides, diagonal):
        base = base_of(chip, core)
        group = chip * 2 + core
        top = group * 128

        def one(j, index):
            ids = ids_a if index < 2 else ids_b
            slot = ids[index % 2, base + j]
            value = (
                sv[index, 0, pl.ds(slot, 1), :] * full[base + j, 0]
                + sv[index, 1, pl.ds(slot, 1), :] * full[base + j, 1]
                + sv[index, 2, pl.ds(slot, 1), :] * full[base + j, 2]
            )
            times = [
                value * factors[index, k, pl.ds(slot, 1), :]
                for k in range(3)
                if (diagonal if k == 0 else sides)
            ]
            return [value] + times

        def fill(k, second):
            row = pl.multiple_of(top + k * 16, 16)
            inner = pl.multiple_of(k * 16, 16)

            def put(high_ref, low_ref, rows, lanes, value):
                high_ref[pl.ds(rows, 16), lanes], low_ref[pl.ds(rows, 16), lanes] = halves(value)

            gathered = 0.0
            for index in range(4):
                lanes = slice(index * EPOCHS, (index + 1) * EPOCHS)
                a = one(2 * k, index)
                b = one(2 * k + 1, index) if second else [jnp.zeros_like(i) for i in a]
                values = [jnp.concatenate([i, j], axis=0) for i, j in zip(a, b)]
                if diagonal:
                    put(u_high, u_low, inner, lanes, values[1])
                if sides:
                    put(f_high, f_low, row, lanes, values[0])
                    put(t_high, t_low, inner, lanes, values[-2])
                    gathered = gathered + values[-1]
            if sides:
                put(t_high, t_low, inner, slice(4 * EPOCHS, 5 * EPOCHS), gathered)

        def step(k, carry):
            fill(k, True)
            return carry

        lax.fori_loop(0, 7, step, 0)
        fill(7, False)
        if sides:
            side = turned(t_high[...], pick[...]) + turned(t_low[...], pick[...])
            rows = pl.ds(pl.multiple_of(top, 128), 128)
            high, low = halves(side * scale)
            high, low = high.astype(F32), low.astype(F32)
            e_left[rows] = jnp.where(lane < 64, high, low).astype(BF16)
            high, low = halves(side * right_scale)
            high, low = high.astype(F32), low.astype(F32)
            e_right[rows] = jnp.where((lane >= 32) & (lane < 64), low, high).astype(BF16)
        if diagonal:
            rows = pl.ds(pl.multiple_of(top, 128), 128)
            v_high, v_low = f_high[rows], f_low[rows]
            own_sum[chip] = squeeze(
                product(u_high[...], u_low[...], u_high[...], u_low[...])
                - product(v_high, v_low, v_high, v_low)
                - turned(e_left[rows], e_right[rows])
            )

    for copy in keeps[1:]:
        copy.wait()
    hand_a.wait()
    local_rows = prepare(0) + prepare(1)
    for copy in swaps:
        copy.wait_recv()
    hand_b = pltpu.make_async_copy(ids_w, ids_b, local.at[8])
    hand_b.start()
    local_rows = local_rows + prepare(2) + prepare(3)
    scale = jnp.where(lane % 32 < 16, lax.rsqrt(local_rows[0:1] + PRIOR), 0.0)
    right_scale = jnp.where(lane % 32 < 16, scale, 1.0)
    special = jnp.where(lane % 32 == 16, -1.0, local_rows[1:2] * scale)
    hand_b.wait()
    build(y, c, True, True)
    mates = [mate_own]
    right_head.wait_recv()
    relay_right = go(4, part(left, head), part(left, head), at_y(right))
    mates.append(go(13, part(left, head), part(left, head), mate))
    left_tail.wait_recv()
    relay_left = go(5, part(right, tail), part(right, tail), at_y(left))
    mates.append(go(14, part(right, tail), part(right, tail), mate))
    mate_own.wait_recv()
    build(y, 1 - c, True, False)
    right_tail.wait_recv()
    mates.append(go(15, part(left, tail), part(left, tail), mate))
    left_head.wait_recv()
    mates.append(go(16, part(right, head), part(right, head), mate))
    build(left, c, True, True)
    build(right, c, True, True)
    for copy in mates[1:]:
        copy.wait_recv()
    build(left, 1 - c, True, False)
    build(right, 1 - c, True, False)
    relay_right.wait_recv()
    mates.append(go(17, part(far, head), part(far, head), mate))
    relay_left.wait_recv()
    mates.append(go(18, part(far, tail), part(far, tail), mate))
    build(far, c, True, False)
    for copy in mates[5:]:
        copy.wait_recv()
    build(far, 1 - c, True, False)

    row = lax.broadcasted_iota(jnp.int32, (8, 128), 0)
    high, low = halves(jnp.where(row == 0, special, 0.0))
    special = jnp.where(lane < 64, high.astype(F32), low.astype(F32))
    e_left[112:128] = jnp.concatenate(
        [e_left[112:128].astype(F32)[0:8], special], axis=0
    ).astype(BF16)

    def multiply(first, count, slabs):
        rows = slice(first * 128, (first + count) * 128)
        own_rows = [pl.ds(pl.multiple_of((slab * 2 + c) * 128, 128), 128) for slab in slabs]
        r_high, r_low, r_side = [
            jnp.concatenate([ref[i] for i in own_rows], axis=0)
            for ref in (f_high, f_low, e_right)
        ]
        result = product(f_high[rows], f_low[rows], r_high, r_low) + turned(e_left[rows], r_side)
        for i, slab in enumerate(slabs):
            lanes = slice(i * 128, (i + 1) * 128)
            for group in range(count):
                for q in range(NX):
                    at = group * 128 + q * 30
                    normal[slab, first + group, q * COVER : (q + 1) * COVER] = -result[
                        at : at + COVER, lanes
                    ]

    def rows_of(peer):
        return pl.ds(pl.multiple_of(peer * COVER, COVER), COVER)

    row_cut = (pl.ds(0, 64), pl.ds(64, 64))

    def y_first(z0):
        return lambda peer, half: normal.at[peer, pl.ds(z0, 2), row_cut[half]]

    def y_then_x(z0):
        return lambda peer, half: y_part.at[pl.ds(z0 + half, 1), rows_of(peer)]

    def x_first(z0):
        return lambda peer, half: normal.at[pl.ds(2 * half, 2), pl.ds(z0, 2), rows_of(peer)]

    def x_then_y(z0):
        return lambda peer, half: x_part.at[peer, pl.ds(z0 - ZA + half, 1)]

    def small_start(base, source, target, me, size, device):
        copies = []
        for k in range(1, size):
            peer = (me + k) % size
            slot = base + k - 1
            copy = remote(
                source(peer), target.at[me], s_send.at[slot], s_recv.at[slot], device(peer)
            )
            copy.start()
            copies.append(copy)
        return copies

    def small_sum(copies, target, me, own, size):
        target[me] = own
        for copy in copies:
            copy.wait_recv()
        result = target[0]
        for k in range(1, size):
            result = result + target[k]
        return result

    def last_copy(peer, slot):
        return remote(
            total.at[peer], arrived.at[slot], z_send.at[peer], z_recv.at[slot], at_z(peer)
        )

    def send_last(peers):
        for peer in peers:
            @pl.when(z != peer)
            def _():
                last_copy(peer, z).start()

    class Ring:
        def __init__(self, number, view, me, device):
            self.number, self.view, self.me, self.device = number, view, me, device
            self.copies = []

        def start(self, slots=(0, 1, 2, 3)):
            self.copies += ring_start(
                self.view, self.me, bufs[self.number], sems[self.number], self.device, slots
            )

        def middle(self):
            self.copies = ring_middle(
                self.view, self.me, bufs[self.number], sems[self.number], self.device, self.copies
            )

        def finish(self, out_0, out_1):
            ring_finish(self.view, self.me, bufs[self.number], self.copies, out_0, out_1)

    firsts = [
        Ring(0, y_first(0), y, at_y),
        Ring(1, y_first(2), y, at_y),
        Ring(2, x_first(4), x, at_x),
        Ring(3, x_first(6), x, at_x),
    ]
    seconds = [
        Ring(4, y_then_x(0), x, at_x),
        Ring(5, y_then_x(2), x, at_x),
        Ring(6, x_then_y(4), y, at_y),
        Ring(7, x_then_y(6), y, at_y),
    ]

    def turn(k):
        z0 = 2 * k
        if z0 < ZA:
            parts = [y_part.at[pl.ds(z0, 2), row_cut[half]] for half in range(2)]
        else:
            parts = [x_part.at[pl.ds(2 * half, 2), pl.ds(z0 - ZA, 2)] for half in range(2)]
        firsts[k].finish(*parts)
        seconds[k].start()

    def close(k):
        seconds[k].finish(total.at[pl.ds(2 * k, 1)], total.at[pl.ds(2 * k + 1, 1)])
        send_last((2 * k, 2 * k + 1))

    multiply(0, 2, (far, right))
    firsts[0].start((0, 1, 2))
    multiply(4, 2, (far, right))
    multiply(4, 2, (left, y))
    firsts[2].start()
    multiply(0, 2, (left, y))
    firsts[0].start((3,))
    multiply(2, 2, (far, right))
    multiply(2, 2, (left, y))
    multiply(6, 2, (far, right))
    multiply(6, 2, (left, y))
    firsts[0].middle()
    firsts[1].start()
    firsts[2].middle()
    firsts[3].start()

    build(far, c, False, True)
    for slab in range(NY):
        small[slab, 0:8] = own_sum[slab]
        small[slab, 8:16] = normal[slab, 0, ROWS : ROWS + 8, :]
    sy = small_start(0, lambda peer: small.at[peer], small_y, y, NY, at_y)

    turn(0)
    turn(2)
    firsts[1].middle()
    firsts[3].middle()
    hold_x[...] = small_sum(sy, small_y, y, small[y], NY)
    sx = small_start(3, lambda peer: hold_x, small_x, x, NX, at_x)
    seconds[0].middle()
    seconds[2].middle()
    turn(1)
    turn(3)
    close(0)
    close(2)
    hold_z[...] = small_sum(sx, small_x, x, hold_x[...], NX)
    sz = small_start(6, lambda peer: hold_z, small_z, z, NZ, at_z)
    seconds[1].middle()
    seconds[3].middle()
    close(1)
    close(3)

    out_small[...] = small_sum(sz, small_z, z, hold_z[...], NZ)
    value = total[z]
    for k in (1, 7, 2, 6, 3, 5, 4):
        peer = (z + k) % NZ
        last_copy(peer, peer).wait_recv()
        value = value + arrived[peer]
    out[...] = value
    sent = [right_head, left_tail, right_tail, left_head, relay_right, relay_left]
    for copies in [sent, swaps, mates, sy, sx, sz] + [ring.copies for ring in firsts + seconds]:
        for copy in copies:
            copy.wait_send()
    for k in range(1, NZ):
        last_copy((z + k) % NZ, z).wait_send()


def finish_kernel(block, sums, owned, right, blocks):
    z, x, y, c = place()
    cross_factor = SATS / math.sqrt(512 * EPOCHS)
    factor = SATS / (512 * SLOTS * EPOCHS)
    value = block[0:30, 0:ROWS]
    row = (z * NX + x) * 30 + lax.broadcasted_iota(jnp.int32, (30, ROWS), 0)
    column = (y * 2 + c) * ROWS + lax.broadcasted_iota(jnp.int32, (30, ROWS), 1)
    owned[...] = jnp.where(row // PAR == column // PAR, 0.0, value) * cross_factor
    right[...] = sums[14:15, 0:ROWS] * factor
    scaled = jnp.broadcast_to((sums[0:8] * factor)[:, None, :], (PAR, PAR, 128))
    place_of = lax.broadcasted_iota(jnp.int32, (PAR, PAR, 128), 2) % PAR
    inner = lax.broadcasted_iota(jnp.int32, (PAR, PAR, 128), 1)
    rows = jnp.where(place_of == inner, scaled, 0.0).reshape(PAR * PAR, 128)
    to = lax.broadcasted_iota(jnp.int32, (128, 128), 0)
    lane = lax.broadcasted_iota(jnp.int32, (128, 128), 1)
    moved = turned(rows, jnp.where(to == lane // PAR, 1.0, 0.0), HIGH)
    blocks[...] = moved.reshape(PAR, PAR, 128)[:, :, 0:OWN]


def ring_buffers(half_0, half_1):
    shapes = [half_0, half_1, half_0, half_1, half_0, half_1, half_0, half_1]
    return [pltpu.VMEM(shape, F32) for shape in shapes]


def shards(sight, mapping, residual, counts, track, knots, orbit):
    shape = jax.ShapeDtypeStruct
    stations = (sight, mapping, residual, counts, knots)
    nb = NZ - ZA
    big = 4 * EPOCHS
    scratch = (
        [pltpu.VMEM(a.shape, a.dtype) for a in stations] * 2
        + [
            pltpu.SMEM((2, SLOTS), jnp.int32),
            pltpu.VMEM((2, 128), jnp.int32),
            pltpu.VMEM((2, 128), jnp.int32),
            pltpu.SMEM((2, 128), jnp.int32),
            pltpu.SMEM((2, 128), jnp.int32),
            pltpu.VMEM((SATS, 3, PAR, EPOCHS), F32),
            pltpu.VMEM((4, 3, SLOTS + 8, EPOCHS), F32),
            pltpu.VMEM((4, 3, SLOTS + 8, EPOCHS), F32),
            pltpu.VMEM((1024, big), BF16),
            pltpu.VMEM((1024, big), BF16),
            pltpu.VMEM((128, big), BF16),
            pltpu.VMEM((128, big), BF16),
            pltpu.VMEM((128, big + EPOCHS), BF16),
            pltpu.VMEM((128, big + EPOCHS), BF16),
            pltpu.VMEM((128, big + EPOCHS), BF16),
            pltpu.VMEM((1024, 128), BF16),
            pltpu.VMEM((1024, 128), BF16),
            pltpu.VMEM((NY, NZ, 128, 128), F32),
            pltpu.VMEM((NY, PAR, 128), F32),
            pltpu.VMEM((NY, 16, 128), F32),
        ]
        + ring_buffers((2, 64, 128), (2, 64, 128)) * 2
        + ring_buffers((2, 2, COVER, 128), (2, 2, COVER, 128)) * 2
        + ring_buffers((1, COVER, 128), (1, COVER, 128)) * 4
        + [
            pltpu.VMEM((ZA, 128, 128), F32),
            pltpu.VMEM((NY, nb, COVER, 128), F32),
            pltpu.VMEM((NZ, COVER, 128), F32),
            pltpu.VMEM((NZ, COVER, 128), F32),
            pltpu.VMEM((NY, 16, 128), F32),
            pltpu.VMEM((NX, 16, 128), F32),
            pltpu.VMEM((NZ, 16, 128), F32),
            pltpu.VMEM((16, 128), F32),
            pltpu.VMEM((16, 128), F32),
            pltpu.SemaphoreType.DMA((19,)),
            pltpu.SemaphoreType.DMA((19,)),
            pltpu.SemaphoreType.DMA((9,)),
        ]
        + [pltpu.SemaphoreType.DMA((6,))] * 16
        + [
            pltpu.SemaphoreType.DMA((NZ,)),
            pltpu.SemaphoreType.DMA((NZ,)),
            pltpu.SemaphoreType.DMA((13,)),
            pltpu.SemaphoreType.DMA((13,)),
        ]
    )
    block, sums = pl.pallas_call(
        main_kernel,
        name="network",
        out_shape=[shape((COVER, 128), F32), shape((16, 128), F32)],
        in_specs=[ANY] * 7,
        out_specs=[VMEM, VMEM],
        scratch_shapes=scratch,
        compiler_params=pltpu.CompilerParams(
            collective_id=0, has_side_effects=True, vmem_limit_bytes=60 * 1024 * 1024
        ),
    )(track, orbit, *stations)

    owned, right, blocks = pl.pallas_call(
        finish_kernel,
        name="finish",
        out_shape=[
            shape((30, ROWS), F32),
            shape((1, ROWS), F32),
            shape((PAR, PAR, OWN), F32),
        ],
        in_specs=[VMEM, VMEM],
        out_specs=[VMEM] * 3,
    )(block, sums)
    return owned.T, right.reshape(ROWS), jnp.transpose(blocks, (2, 0, 1))


def solution(mesh):
    placed = (
        P(("sta", "sat"), None, None, None),
        P(("sta", "sat"), None, None),
        P(("sta", "sat"), None, None),
        P(("sta", "sat"), None, None),
        P(("sta", "sat"), None),
        P(("sta", "sat"), None),
        P("sat", None, None, None),
    )
    return jax.shard_map(
        shards,
        mesh=mesh,
        in_specs=placed,
        out_specs=(P("sat", "sta"), P("sat"), P("sat", None, None)),
        check_vma=False,
    )
```

```python
import functools
import math

import jax
import jax.numpy as jnp
from jax import lax
from jax.experimental import pallas as pl
from jax.experimental.pallas import tpu as pltpu
from jax.sharding import PartitionSpec as P

F32 = jnp.float32
BF16 = jnp.bfloat16
MESH = pl.DeviceIdType.MESH
HIGH = lax.Precision.HIGHEST

SATS = 120
OWN = 15
PAR = 8
SLOTS = 32
EPOCHS = 256
KNOTS = 4
PRIOR = 1.0
NY = 4
NX = 4
NZ = 8
ROWS = 120
COVER = 32
HEAD = (0, 5)
TAIL = (5, 4)
REST = (9, 6)
ZA = 4
ANY = pl.BlockSpec(memory_space=pl.ANY)
VMEM = pl.BlockSpec(memory_space=pltpu.VMEM)
SMEM = pl.BlockSpec(memory_space=pltpu.SMEM)


def place():
    sta = lax.axis_index("sta")
    sat = lax.axis_index("sat")
    return sta // NX, sta % NX, sat // 2, sat % 2


def remote(src, dst, send, recv, device):
    return pltpu.make_async_remote_copy(
        src_ref=src,
        dst_ref=dst,
        send_sem=send,
        recv_sem=recv,
        device_id=device,
        device_id_type=MESH,
    )


def greet(peers):
    barrier = pltpu.get_barrier_semaphore()
    for peer in peers:
        pl.semaphore_signal(barrier, inc=1, device_id=peer, device_id_type=MESH)
    pl.semaphore_wait(barrier, len(peers))


def halves(value):
    high = value.astype(BF16)
    low = (value - high.astype(F32)).astype(BF16)
    return high, low


def turned(a, b, precision=None):
    return lax.dot_general(
        a, b, (((1,), (1,)), ((), ())), preferred_element_type=F32, precision=precision
    )


def product(a_high, a_low, b_high, b_low):
    return turned(a_high, b_high) + turned(a_high, b_low) + turned(a_low, b_high)


def ring_start(view, me, buffers, sems, device, slots):
    far, right, left = (me + 2) % 4, (me + 1) % 4, (me + 3) % 4
    b_0, b_1, l_0, l_1, r_0, r_1 = buffers[:6]
    send, recv = sems
    plan = (
        (view(far, 0), b_0, right),
        (view(far, 1), b_1, left),
        (view(right, 1), l_1, right),
        (view(left, 0), r_0, left),
    )
    copies = []
    for slot in slots:
        src, dst, peer = plan[slot]
        copy = remote(src, dst, send.at[slot], recv.at[slot], device(peer))
        copy.start()
        copies.append(copy)
    return copies


def ring_middle(view, me, buffers, sems, device, copies):
    right, left = (me + 1) % 4, (me + 3) % 4
    b_0, b_1, l_0, l_1, r_0, r_1, s_0, s_1 = buffers
    send, recv = sems
    copies[0].wait_recv()
    s_0[...] = view(right, 0)[...] + b_0[...]
    one = remote(s_0, l_0, send.at[4], recv.at[4], device(right))
    one.start()
    copies[1].wait_recv()
    s_1[...] = view(left, 1)[...] + b_1[...]
    two = remote(s_1, r_1, send.at[5], recv.at[5], device(left))
    two.start()
    return copies + [one, two]


def ring_finish(view, me, buffers, copies, out_0, out_1):
    b_0, b_1, l_0, l_1, r_0, r_1 = buffers[:6]
    for index in (2, 3, 4, 5):
        copies[index].wait_recv()
    out_0[...] = view(me, 0)[...] + l_0[...] + r_0[...]
    out_1[...] = view(me, 1)[...] + l_1[...] + r_1[...]


def main_kernel(*refs):
    track, orbit = refs[0:2]
    given = refs[2:7]
    out, out_small = refs[7:9]
    refs = refs[9:]
    mine, other, refs = refs[:5], refs[5:10], refs[10:]
    (track_s, ids_v, ids_w, ids_a, ids_b, full, sv, factors, f_high, f_low, u_high, u_low,
     t_high, t_low, pick, e_left, e_right, normal, own_sum, small), refs = refs[:20], refs[20:]
    bufs, refs = [refs[i * 8 : (i + 1) * 8] for i in range(8)], refs[64:]
    (y_part, x_part, total, arrived, small_y, small_x, small_z, hold_x, hold_z), refs = (
        refs[:9], refs[9:])
    g_send, g_recv, local = refs[:3]
    refs = refs[3:]
    sems = [(refs[2 * i], refs[2 * i + 1]) for i in range(8)]
    z_send, z_recv, s_send, s_recv = refs[16:]
    z, x, y, c = place()

    def at_y(peer):
        return (z * NX + x, peer * 2 + c)

    def at_x(peer):
        return (z * NX + peer, y * 2 + c)

    def at_z(peer):
        return (peer * NX + x, y * 2 + c)

    mate = (z * NX + x, y * 2 + 1 - c)
    far, right, left = (y + 2) % NY, (y + 1) % NY, (y + 3) % NY
    twin = at_x(x + 1 - 2 * (x % 2))
    share, share_twin = (REST[0] + 3 * (x % 2), 3), (REST[0] + 3 - 3 * (x % 2), 3)

    def base_of(chip, core):
        return (chip * 2 + core) * OWN

    def part(chip, cut):
        return full.at[pl.ds(base_of(chip, c) + cut[0], cut[1])]

    def own(cut):
        return orbit.at[pl.ds(cut[0], cut[1])]

    keeps = [
        pltpu.make_async_copy(a, b, local.at[i])
        for i, (a, b) in enumerate(
            zip(
                (track,) + given + (orbit,),
                (track_s,) + mine + (full.at[pl.ds(base_of(y, c), OWN)],),
            )
        )
    ]
    for copy in keeps:
        copy.start()

    greet(
        [at_y((y + k) % NY) for k in range(1, NY)]
        + [at_x((x + k) % NX) for k in range(1, NX)]
        + [at_z((z + k) % NZ) for k in range(1, NZ)]
        + [mate]
    )

    everything = []

    def go(src, dst, device):
        slot = len(everything)
        copy = remote(src, dst, g_send.at[slot], g_recv.at[slot], device)
        copy.start()
        everything.append(copy)
        return copy

    def pass_on(chip, cut, device):
        return go(part(chip, cut), part(chip, cut), device)

    share_right = go(own(share), part(y, share), at_y(right))
    share_left = go(own(share), part(y, share), at_y(left))
    head_right = go(own(HEAD), part(y, HEAD), at_y(right))
    tail_left = go(own(TAIL), part(y, TAIL), at_y(left))
    swaps = [go(a, b, mate) for a, b in zip(given, other)]
    mate_own = go(orbit, full.at[pl.ds(base_of(y, c), OWN)], mate)

    keeps[0].wait()
    place_lane = lax.broadcasted_iota(jnp.int32, (1, 128), 1)
    for s in range(2):
        slots = jnp.full((1, 128), SLOTS, jnp.int32)
        for m in range(SLOTS):
            slots = jnp.where(place_lane == track_s[s, m], m, slots)
        ids_v[s : s + 1, :] = slots
    hand_a = pltpu.make_async_copy(ids_v, ids_a, local.at[7])
    hand_a.start()
    swaps.append(go(ids_v, ids_w, mate))

    blank = jnp.zeros((4, 3, 8, EPOCHS), F32)
    sv[:, :, SLOTS:, :] = blank
    factors[:, :, SLOTS:, :] = blank
    lane_rows = lax.broadcasted_iota(jnp.int32, (128, EPOCHS), 0)
    row8 = lax.broadcasted_iota(jnp.int32, (8, EPOCHS), 0)
    pick_last = jnp.where((lane_rows % 32 == 16) & (lane_rows < 96), 1.0, 0.0).astype(BF16)

    pick[:, 4 * EPOCHS :] = pick_last

    def prepare(index):
        sight, mapping, residual, counts, knots = mine if index < 2 else other
        s = index % 2
        chosen = lane_rows % 32 == knots[s : s + 1, :] + KNOTS * index
        chosen = jnp.where(chosen & (lane_rows < 96), 1.0, 0.0)
        wide = EPOCHS * index
        pick[:, wide : wide + EPOCHS] = chosen.astype(BF16)
        weight = counts[s].astype(F32)
        path = mapping[s]
        seen = residual[s]
        shared = jnp.maximum(jnp.sum(weight, 0, keepdims=True), 1.0)
        share = 1.0 / shared
        root = lax.rsqrt(shared)
        grow = shared * root
        weight_map = weight * path
        sum_map = jnp.sum(weight_map, 0, keepdims=True)
        sum_res = jnp.sum(weight * seen, 0, keepdims=True)
        scaled = weight * root
        for k in range(3):
            sv[index, k, 0:SLOTS] = sight[s, k] * scaled
        factors[index, 0, 0:SLOTS] = jnp.where(
            weight > 0.0, lax.rsqrt(jnp.maximum(weight, 1.0)) * grow, 0.0
        )
        factors[index, 1, 0:SLOTS] = (path - sum_map * share) * grow
        factors[index, 2, 0:SLOTS] = (seen - sum_res * share) * grow
        square = jnp.sum(weight_map * path, 0, keepdims=True) - sum_map * sum_map * share
        cross = jnp.sum(weight_map * seen, 0, keepdims=True) - sum_map * sum_res * share
        pair = jnp.where(row8 == 0, square, jnp.where(row8 == 1, cross, 0.0))
        return turned(pair, chosen, HIGH)

    own_row = lax.broadcasted_iota(jnp.int32, (128, 128), 0) // PAR
    own_lane = lax.broadcasted_iota(jnp.int32, (128, 128), 1) // PAR
    lane = lax.broadcasted_iota(jnp.int32, (1, 128), 1)

    def squeeze(block):
        block = jnp.where(own_row == own_lane, block, 0.0)
        return jnp.sum(block.reshape(16, PAR, 128), 0)

    def build(chip, core, sides, diagonal):
        base = base_of(chip, core)
        group = chip * 2 + core
        top = group * 128

        def one(j, index):
            ids = ids_a if index < 2 else ids_b
            slot = ids[index % 2, base + j]
            value = (
                sv[index, 0, pl.ds(slot, 1), :] * full[base + j, 0]
                + sv[index, 1, pl.ds(slot, 1), :] * full[base + j, 1]
                + sv[index, 2, pl.ds(slot, 1), :] * full[base + j, 2]
            )
            times = [
                value * factors[index, k, pl.ds(slot, 1), :]
                for k in range(3)
                if (diagonal if k == 0 else sides)
            ]
            return [value] + times

        def fill(k, second):
            row = pl.multiple_of(top + k * 16, 16)
            inner = pl.multiple_of(k * 16, 16)

            def put(high_ref, low_ref, rows, lanes, value):
                high_ref[pl.ds(rows, 16), lanes], low_ref[pl.ds(rows, 16), lanes] = halves(value)

            gathered = 0.0
            for index in range(4):
                lanes = slice(index * EPOCHS, (index + 1) * EPOCHS)
                a = one(2 * k, index)
                b = one(2 * k + 1, index) if second else [jnp.zeros_like(i) for i in a]
                values = [jnp.concatenate([i, j], axis=0) for i, j in zip(a, b)]
                if diagonal:
                    put(u_high, u_low, inner, lanes, values[1])
                if sides:
                    put(f_high, f_low, row, lanes, values[0])
                    put(t_high, t_low, inner, lanes, values[-2])
                    gathered = gathered + values[-1]
            if sides:
                put(t_high, t_low, inner, slice(4 * EPOCHS, 5 * EPOCHS), gathered)

        def step(k, carry):
            fill(k, True)
            return carry

        lax.fori_loop(0, 7, step, 0)
        fill(7, False)
        if sides:
            side = turned(t_high[...], pick[...]) + turned(t_low[...], pick[...])
            rows = pl.ds(pl.multiple_of(top, 128), 128)
            high, low = halves(side * scale)
            high, low = high.astype(F32), low.astype(F32)
            e_left[rows] = jnp.where(lane < 64, high, low).astype(BF16)
            high, low = halves(side * right_scale)
            high, low = high.astype(F32), low.astype(F32)
            e_right[rows] = jnp.where((lane >= 32) & (lane < 64), low, high).astype(BF16)
        if diagonal:
            rows = pl.ds(pl.multiple_of(top, 128), 128)
            v_high, v_low = f_high[rows], f_low[rows]
            own_sum[chip] = squeeze(
                product(u_high[...], u_low[...], u_high[...], u_low[...])
                - product(v_high, v_low, v_high, v_low)
                - turned(e_left[rows], e_right[rows])
            )

    for copy in keeps[1:]:
        copy.wait()
    hand_a.wait()
    local_rows = prepare(0) + prepare(1)
    for copy in swaps:
        copy.wait_recv()
    hand_b = pltpu.make_async_copy(ids_w, ids_b, local.at[8])
    hand_b.start()
    local_rows = local_rows + prepare(2) + prepare(3)
    scale = jnp.where(lane % 32 < 16, lax.rsqrt(local_rows[0:1] + PRIOR), 0.0)
    right_scale = jnp.where(lane % 32 < 16, scale, 1.0)
    special = jnp.where(lane % 32 == 16, -1.0, local_rows[1:2] * scale)
    hand_b.wait()
    first, second = (share[0], 2), (share[0] + 2, 1)
    share_right.wait_recv()
    far_first = pass_on(left, first, at_y(right))
    twin_left = pass_on(left, share, twin)
    share_left.wait_recv()
    far_second = pass_on(right, second, at_y(left))
    twin_right = pass_on(right, share, twin)
    tail_right = go(own(TAIL), part(y, TAIL), at_y(right))
    head_left = go(own(HEAD), part(y, HEAD), at_y(left))
    build(y, c, True, True)

    head_right.wait_recv()
    far_head = pass_on(left, HEAD, at_y(right))
    mates_left = [pass_on(left, HEAD, mate)]
    tail_left.wait_recv()
    far_tail = pass_on(right, TAIL, at_y(left))
    mates_right = [pass_on(right, TAIL, mate)]
    far_first.wait_recv()
    far_second.wait_recv()
    twin_far = pass_on(far, share, twin)
    mates_far = [pass_on(far, share, mate)]
    twin_left.wait_recv()
    mates_left.append(pass_on(left, REST, mate))
    twin_right.wait_recv()
    mates_right.append(pass_on(right, REST, mate))
    mate_own.wait_recv()
    build(y, 1 - c, True, False)
    tail_right.wait_recv()
    mates_left.append(pass_on(left, TAIL, mate))
    head_left.wait_recv()
    mates_right.append(pass_on(right, HEAD, mate))
    build(left, c, True, True)
    twin_far.wait_recv()
    mates_far.append(pass_on(far, share_twin, mate))
    build(right, c, True, True)
    far_head.wait_recv()
    mates_far.append(pass_on(far, HEAD, mate))
    far_tail.wait_recv()
    mates_far.append(pass_on(far, TAIL, mate))
    for copy in mates_left:
        copy.wait_recv()
    build(left, 1 - c, True, False)
    for copy in mates_right:
        copy.wait_recv()
    build(right, 1 - c, True, False)
    build(far, c, True, False)
    for copy in mates_far:
        copy.wait_recv()
    build(far, 1 - c, True, False)

    row = lax.broadcasted_iota(jnp.int32, (8, 128), 0)
    high, low = halves(jnp.where(row == 0, special, 0.0))
    special = jnp.where(lane < 64, high.astype(F32), low.astype(F32))
    e_left[112:128] = jnp.concatenate(
        [e_left[112:128].astype(F32)[0:8], special], axis=0
    ).astype(BF16)

    def multiply(first, count, slabs):
        rows = slice(first * 128, (first + count) * 128)
        own_rows = [pl.ds(pl.multiple_of((slab * 2 + c) * 128, 128), 128) for slab in slabs]
        r_high, r_low, r_side = [
            jnp.concatenate([ref[i] for i in own_rows], axis=0)
            for ref in (f_high, f_low, e_right)
        ]
        result = product(f_high[rows], f_low[rows], r_high, r_low) + turned(e_left[rows], r_side)
        for i, slab in enumerate(slabs):
            lanes = slice(i * 128, (i + 1) * 128)
            for group in range(count):
                for q in range(NX):
                    at = group * 128 + q * 30
                    normal[slab, first + group, q * COVER : (q + 1) * COVER] = -result[
                        at : at + COVER, lanes
                    ]

    def rows_of(peer):
        return pl.ds(pl.multiple_of(peer * COVER, COVER), COVER)

    row_cut = (pl.ds(0, 64), pl.ds(64, 64))

    def y_first(z0):
        return lambda peer, half: normal.at[peer, pl.ds(z0, 2), row_cut[half]]

    def y_then_x(z0):
        return lambda peer, half: y_part.at[pl.ds(z0 + half, 1), rows_of(peer)]

    def x_first(z0):
        return lambda peer, half: normal.at[pl.ds(2 * half, 2), pl.ds(z0, 2), rows_of(peer)]

    def x_then_y(z0):
        return lambda peer, half: x_part.at[peer, pl.ds(z0 - ZA + half, 1)]

    def small_start(base, source, target, me, size, device):
        copies = []
        for k in range(1, size):
            peer = (me + k) % size
            slot = base + k - 1
            copy = remote(
                source(peer), target.at[me], s_send.at[slot], s_recv.at[slot], device(peer)
            )
            copy.start()
            copies.append(copy)
        return copies

    def small_sum(copies, target, me, own, size):
        target[me] = own
        for copy in copies:
            copy.wait_recv()
        result = target[0]
        for k in range(1, size):
            result = result + target[k]
        return result

    def last_copy(peer, slot):
        return remote(
            total.at[peer], arrived.at[slot], z_send.at[peer], z_recv.at[slot], at_z(peer)
        )

    def send_last(peers):
        for peer in peers:
            @pl.when(z != peer)
            def _():
                last_copy(peer, z).start()

    class Ring:
        def __init__(self, number, view, me, device):
            self.number, self.view, self.me, self.device = number, view, me, device
            self.copies = []

        def start(self, slots=(0, 1, 2, 3)):
            self.copies += ring_start(
                self.view, self.me, bufs[self.number], sems[self.number], self.device, slots
            )

        def middle(self):
            self.copies = ring_middle(
                self.view, self.me, bufs[self.number], sems[self.number], self.device, self.copies
            )

        def finish(self, out_0, out_1):
            ring_finish(self.view, self.me, bufs[self.number], self.copies, out_0, out_1)

    firsts = [
        Ring(0, y_first(0), y, at_y),
        Ring(1, y_first(2), y, at_y),
        Ring(2, x_first(4), x, at_x),
        Ring(3, x_first(6), x, at_x),
    ]
    seconds = [
        Ring(4, y_then_x(0), x, at_x),
        Ring(5, y_then_x(2), x, at_x),
        Ring(6, x_then_y(4), y, at_y),
        Ring(7, x_then_y(6), y, at_y),
    ]

    def turn(k):
        z0 = 2 * k
        if z0 < ZA:
            parts = [y_part.at[pl.ds(z0, 2), row_cut[half]] for half in range(2)]
        else:
            parts = [x_part.at[pl.ds(2 * half, 2), pl.ds(z0 - ZA, 2)] for half in range(2)]
        firsts[k].finish(*parts)
        seconds[k].start()

    def close(k):
        seconds[k].finish(total.at[pl.ds(2 * k, 1)], total.at[pl.ds(2 * k + 1, 1)])
        send_last((2 * k, 2 * k + 1))

    multiply(0, 2, (far, right))
    firsts[0].start((0, 1, 2))
    multiply(4, 2, (far, right))
    multiply(4, 2, (left, y))
    firsts[2].start()
    multiply(0, 2, (left, y))
    firsts[0].start((3,))
    multiply(2, 2, (far, right))
    multiply(2, 2, (left, y))
    multiply(6, 2, (far, right))
    multiply(6, 2, (left, y))
    firsts[0].middle()
    firsts[1].start()
    firsts[2].middle()
    firsts[3].start()

    build(far, c, False, True)
    for slab in range(NY):
        small[slab, 0:8] = own_sum[slab]
        small[slab, 8:16] = normal[slab, 0, ROWS : ROWS + 8, :]
    sy = small_start(0, lambda peer: small.at[peer], small_y, y, NY, at_y)

    turn(0)
    turn(2)
    firsts[1].middle()
    firsts[3].middle()
    hold_x[...] = small_sum(sy, small_y, y, small[y], NY)
    sx = small_start(3, lambda peer: hold_x, small_x, x, NX, at_x)
    seconds[0].middle()
    seconds[2].middle()
    turn(1)
    turn(3)
    close(0)
    close(2)
    hold_z[...] = small_sum(sx, small_x, x, hold_x[...], NX)
    sz = small_start(6, lambda peer: hold_z, small_z, z, NZ, at_z)
    seconds[1].middle()
    seconds[3].middle()
    close(1)
    close(3)

    out_small[...] = small_sum(sz, small_z, z, hold_z[...], NZ)
    value = total[z]
    for k in (1, 7, 2, 6, 3, 5, 4):
        peer = (z + k) % NZ
        last_copy(peer, peer).wait_recv()
        value = value + arrived[peer]
    out[...] = value
    for copies in [everything, sy, sx, sz] + [ring.copies for ring in firsts + seconds]:
        for copy in copies:
            copy.wait_send()
    for k in range(1, NZ):
        last_copy((z + k) % NZ, z).wait_send()


def finish_kernel(block, sums, owned, right, blocks):
    z, x, y, c = place()
    cross_factor = SATS / math.sqrt(512 * EPOCHS)
    factor = SATS / (512 * SLOTS * EPOCHS)
    value = block[0:30, 0:ROWS]
    row = (z * NX + x) * 30 + lax.broadcasted_iota(jnp.int32, (30, ROWS), 0)
    column = (y * 2 + c) * ROWS + lax.broadcasted_iota(jnp.int32, (30, ROWS), 1)
    owned[...] = jnp.where(row // PAR == column // PAR, 0.0, value) * cross_factor
    right[...] = sums[14:15, 0:ROWS] * factor
    scaled = jnp.broadcast_to((sums[0:8] * factor)[:, None, :], (PAR, PAR, 128))
    place_of = lax.broadcasted_iota(jnp.int32, (PAR, PAR, 128), 2) % PAR
    inner = lax.broadcasted_iota(jnp.int32, (PAR, PAR, 128), 1)
    rows = jnp.where(place_of == inner, scaled, 0.0).reshape(PAR * PAR, 128)
    to = lax.broadcasted_iota(jnp.int32, (128, 128), 0)
    lane = lax.broadcasted_iota(jnp.int32, (128, 128), 1)
    moved = turned(rows, jnp.where(to == lane // PAR, 1.0, 0.0), HIGH)
    blocks[...] = moved.reshape(PAR, PAR, 128)[:, :, 0:OWN]


def ring_buffers(half_0, half_1):
    shapes = [half_0, half_1, half_0, half_1, half_0, half_1, half_0, half_1]
    return [pltpu.VMEM(shape, F32) for shape in shapes]


def shards(sight, mapping, residual, counts, track, knots, orbit):
    shape = jax.ShapeDtypeStruct
    stations = (sight, mapping, residual, counts, knots)
    nb = NZ - ZA
    big = 4 * EPOCHS
    scratch = (
        [pltpu.VMEM(a.shape, a.dtype) for a in stations] * 2
        + [
            pltpu.SMEM((2, SLOTS), jnp.int32),
            pltpu.VMEM((2, 128), jnp.int32),
            pltpu.VMEM((2, 128), jnp.int32),
            pltpu.SMEM((2, 128), jnp.int32),
            pltpu.SMEM((2, 128), jnp.int32),
            pltpu.VMEM((SATS, 3, PAR, EPOCHS), F32),
            pltpu.VMEM((4, 3, SLOTS + 8, EPOCHS), F32),
            pltpu.VMEM((4, 3, SLOTS + 8, EPOCHS), F32),
            pltpu.VMEM((1024, big), BF16),
            pltpu.VMEM((1024, big), BF16),
            pltpu.VMEM((128, big), BF16),
            pltpu.VMEM((128, big), BF16),
            pltpu.VMEM((128, big + EPOCHS), BF16),
            pltpu.VMEM((128, big + EPOCHS), BF16),
            pltpu.VMEM((128, big + EPOCHS), BF16),
            pltpu.VMEM((1024, 128), BF16),
            pltpu.VMEM((1024, 128), BF16),
            pltpu.VMEM((NY, NZ, 128, 128), F32),
            pltpu.VMEM((NY, PAR, 128), F32),
            pltpu.VMEM((NY, 16, 128), F32),
        ]
        + ring_buffers((2, 64, 128), (2, 64, 128)) * 2
        + ring_buffers((2, 2, COVER, 128), (2, 2, COVER, 128)) * 2
        + ring_buffers((1, COVER, 128), (1, COVER, 128)) * 4
        + [
            pltpu.VMEM((ZA, 128, 128), F32),
            pltpu.VMEM((NY, nb, COVER, 128), F32),
            pltpu.VMEM((NZ, COVER, 128), F32),
            pltpu.VMEM((NZ, COVER, 128), F32),
            pltpu.VMEM((NY, 16, 128), F32),
            pltpu.VMEM((NX, 16, 128), F32),
            pltpu.VMEM((NZ, 16, 128), F32),
            pltpu.VMEM((16, 128), F32),
            pltpu.VMEM((16, 128), F32),
            pltpu.SemaphoreType.DMA((30,)),
            pltpu.SemaphoreType.DMA((30,)),
            pltpu.SemaphoreType.DMA((9,)),
        ]
        + [pltpu.SemaphoreType.DMA((6,))] * 16
        + [
            pltpu.SemaphoreType.DMA((NZ,)),
            pltpu.SemaphoreType.DMA((NZ,)),
            pltpu.SemaphoreType.DMA((13,)),
            pltpu.SemaphoreType.DMA((13,)),
        ]
    )
    block, sums = pl.pallas_call(
        main_kernel,
        name="network",
        out_shape=[shape((COVER, 128), F32), shape((16, 128), F32)],
        in_specs=[ANY] * 7,
        out_specs=[VMEM, VMEM],
        scratch_shapes=scratch,
        compiler_params=pltpu.CompilerParams(
            collective_id=0, has_side_effects=True, vmem_limit_bytes=60 * 1024 * 1024
        ),
    )(track, orbit, *stations)

    owned, right, blocks = pl.pallas_call(
        finish_kernel,
        name="finish",
        out_shape=[
            shape((30, ROWS), F32),
            shape((1, ROWS), F32),
            shape((PAR, PAR, OWN), F32),
        ],
        in_specs=[VMEM, VMEM],
        out_specs=[VMEM] * 3,
    )(block, sums)
    return owned.T, right.reshape(ROWS), jnp.transpose(blocks, (2, 0, 1))


def solution(mesh):
    placed = (
        P(("sta", "sat"), None, None, None),
        P(("sta", "sat"), None, None),
        P(("sta", "sat"), None, None),
        P(("sta", "sat"), None, None),
        P(("sta", "sat"), None),
        P(("sta", "sat"), None),
        P("sat", None, None, None),
    )
    return jax.shard_map(
        shards,
        mesh=mesh,
        in_specs=placed,
        out_specs=(P("sat", "sta"), P("sat"), P("sat", None, None)),
        check_vma=False,
    )
```

```python
import functools
import math

import jax
import jax.numpy as jnp
from jax import lax
from jax.experimental import pallas as pl
from jax.experimental.pallas import tpu as pltpu
from jax.sharding import PartitionSpec as P

F32 = jnp.float32
BF16 = jnp.bfloat16
MESH = pl.DeviceIdType.MESH
HIGH = lax.Precision.HIGHEST

SATS = 120
OWN = 15
PAR = 8
SLOTS = 32
EPOCHS = 256
KNOTS = 4
PRIOR = 1.0
NY = 4
NX = 4
NZ = 8
ROWS = 120
COVER = 32
HEAD = (0, 5)
TAIL = (5, 4)
REST = (9, 6)
ZA = 4
ANY = pl.BlockSpec(memory_space=pl.ANY)
VMEM = pl.BlockSpec(memory_space=pltpu.VMEM)
SMEM = pl.BlockSpec(memory_space=pltpu.SMEM)


def place():
    sta = lax.axis_index("sta")
    sat = lax.axis_index("sat")
    return sta // NX, sta % NX, sat // 2, sat % 2


def remote(src, dst, send, recv, device):
    return pltpu.make_async_remote_copy(
        src_ref=src,
        dst_ref=dst,
        send_sem=send,
        recv_sem=recv,
        device_id=device,
        device_id_type=MESH,
    )


def greet(peers):
    barrier = pltpu.get_barrier_semaphore()
    for peer in peers:
        pl.semaphore_signal(barrier, inc=1, device_id=peer, device_id_type=MESH)
    pl.semaphore_wait(barrier, len(peers))


def halves(value):
    high = value.astype(BF16)
    low = (value - high.astype(F32)).astype(BF16)
    return high, low


def turned(a, b, precision=None):
    return lax.dot_general(
        a, b, (((1,), (1,)), ((), ())), preferred_element_type=F32, precision=precision
    )


def product(a_high, a_low, b_high, b_low):
    return turned(a_high, b_high) + turned(a_high, b_low) + turned(a_low, b_high)


def ring_start(view, me, buffers, sems, device, slots):
    far, right, left = (me + 2) % 4, (me + 1) % 4, (me + 3) % 4
    b_0, b_1, l_0, l_1, r_0, r_1 = buffers[:6]
    send, recv = sems
    plan = (
        (view(far, 0), b_0, right),
        (view(far, 1), b_1, left),
        (view(right, 1), l_1, right),
        (view(left, 0), r_0, left),
    )
    copies = []
    for slot in slots:
        src, dst, peer = plan[slot]
        copy = remote(src, dst, send.at[slot], recv.at[slot], device(peer))
        copy.start()
        copies.append(copy)
    return copies


def ring_middle(view, me, buffers, sems, device, copies):
    right, left = (me + 1) % 4, (me + 3) % 4
    b_0, b_1, l_0, l_1, r_0, r_1, s_0, s_1 = buffers
    send, recv = sems
    copies[0].wait_recv()
    s_0[...] = view(right, 0)[...] + b_0[...]
    one = remote(s_0, l_0, send.at[4], recv.at[4], device(right))
    one.start()
    copies[1].wait_recv()
    s_1[...] = view(left, 1)[...] + b_1[...]
    two = remote(s_1, r_1, send.at[5], recv.at[5], device(left))
    two.start()
    return copies + [one, two]


def ring_finish(view, me, buffers, copies, out_0, out_1):
    b_0, b_1, l_0, l_1, r_0, r_1 = buffers[:6]
    for index in (2, 3, 4, 5):
        copies[index].wait_recv()
    out_0[...] = view(me, 0)[...] + l_0[...] + r_0[...]
    out_1[...] = view(me, 1)[...] + l_1[...] + r_1[...]


def main_kernel(*refs):
    track, orbit = refs[0:2]
    given = refs[2:7]
    out, out_small = refs[7:9]
    refs = refs[9:]
    mine, other, refs = refs[:5], refs[5:10], refs[10:]
    (track_s, ids_v, ids_w, ids_a, ids_b, full, sv, factors, f_high, f_low, u_high, u_low,
     t_high, t_low, pick, e_left, e_right, normal, own_sum, small), refs = refs[:20], refs[20:]
    bufs, refs = [refs[i * 8 : (i + 1) * 8] for i in range(8)], refs[64:]
    (y_part, x_part, total, arrived, small_y, small_x, small_z, hold_x, hold_z), refs = (
        refs[:9], refs[9:])
    g_send, g_recv, local = refs[:3]
    refs = refs[3:]
    sems = [(refs[2 * i], refs[2 * i + 1]) for i in range(8)]
    z_send, z_recv, s_send, s_recv = refs[16:]
    z, x, y, c = place()

    def at_y(peer):
        return (z * NX + x, peer * 2 + c)

    def at_x(peer):
        return (z * NX + peer, y * 2 + c)

    def at_z(peer):
        return (peer * NX + x, y * 2 + c)

    mate = (z * NX + x, y * 2 + 1 - c)
    far, right, left = (y + 2) % NY, (y + 1) % NY, (y + 3) % NY
    twin = at_x(x + 1 - 2 * (x % 2))
    share, share_twin = (REST[0] + 3 * (x % 2), 3), (REST[0] + 3 - 3 * (x % 2), 3)

    def base_of(chip, core):
        return (chip * 2 + core) * OWN

    def part(chip, cut):
        return full.at[pl.ds(base_of(chip, c) + cut[0], cut[1])]

    def own(cut):
        return orbit.at[pl.ds(cut[0], cut[1])]

    keeps = [
        pltpu.make_async_copy(a, b, local.at[i])
        for i, (a, b) in enumerate(
            zip(
                (track,) + given + (orbit,),
                (track_s,) + mine + (full.at[pl.ds(base_of(y, c), OWN)],),
            )
        )
    ]
    for copy in keeps:
        copy.start()

    greet(
        [at_y((y + k) % NY) for k in range(1, NY)]
        + [at_x((x + k) % NX) for k in range(1, NX)]
        + [at_z((z + k) % NZ) for k in range(1, NZ)]
        + [mate]
    )

    everything = []

    def go(src, dst, device):
        slot = len(everything)
        copy = remote(src, dst, g_send.at[slot], g_recv.at[slot], device)
        copy.start()
        everything.append(copy)
        return copy

    def pass_on(chip, cut, device):
        return go(part(chip, cut), part(chip, cut), device)

    share_right = go(own(share), part(y, share), at_y(right))
    share_left = go(own(share), part(y, share), at_y(left))
    head_right = go(own(HEAD), part(y, HEAD), at_y(right))
    tail_left = go(own(TAIL), part(y, TAIL), at_y(left))
    swaps = [go(a, b, mate) for a, b in zip(given, other)]
    mate_own = go(orbit, full.at[pl.ds(base_of(y, c), OWN)], mate)

    keeps[0].wait()
    place_lane = lax.broadcasted_iota(jnp.int32, (1, 128), 1)
    for s in range(2):
        slots = jnp.full((1, 128), SLOTS, jnp.int32)
        for m in range(SLOTS):
            slots = jnp.where(place_lane == track_s[s, m], m, slots)
        ids_v[s : s + 1, :] = slots
    hand_a = pltpu.make_async_copy(ids_v, ids_a, local.at[7])
    hand_a.start()
    swaps.append(go(ids_v, ids_w, mate))

    blank = jnp.zeros((4, 3, 8, EPOCHS), F32)
    sv[:, :, SLOTS:, :] = blank
    factors[:, :, SLOTS:, :] = blank
    lane_rows = lax.broadcasted_iota(jnp.int32, (128, EPOCHS), 0)
    row8 = lax.broadcasted_iota(jnp.int32, (8, EPOCHS), 0)
    pick_last = jnp.where((lane_rows % 32 == 16) & (lane_rows < 96), 1.0, 0.0).astype(BF16)

    pick[:, 4 * EPOCHS :] = pick_last

    def prepare(index):
        sight, mapping, residual, counts, knots = mine if index < 2 else other
        s = index % 2
        chosen = lane_rows % 32 == knots[s : s + 1, :] + KNOTS * index
        chosen = jnp.where(chosen & (lane_rows < 96), 1.0, 0.0)
        wide = EPOCHS * index
        pick[:, wide : wide + EPOCHS] = chosen.astype(BF16)
        weight = counts[s].astype(F32)
        path = mapping[s]
        seen = residual[s]
        shared = jnp.maximum(jnp.sum(weight, 0, keepdims=True), 1.0)
        share = 1.0 / shared
        root = lax.rsqrt(shared)
        grow = shared * root
        weight_map = weight * path
        sum_map = jnp.sum(weight_map, 0, keepdims=True)
        sum_res = jnp.sum(weight * seen, 0, keepdims=True)
        scaled = weight * root
        for k in range(3):
            sv[index, k, 0:SLOTS] = sight[s, k] * scaled
        factors[index, 0, 0:SLOTS] = jnp.where(
            weight > 0.0, lax.rsqrt(jnp.maximum(weight, 1.0)) * grow, 0.0
        )
        factors[index, 1, 0:SLOTS] = (path - sum_map * share) * grow
        factors[index, 2, 0:SLOTS] = (seen - sum_res * share) * grow
        square = jnp.sum(weight_map * path, 0, keepdims=True) - sum_map * sum_map * share
        cross = jnp.sum(weight_map * seen, 0, keepdims=True) - sum_map * sum_res * share
        pair = jnp.where(row8 == 0, square, jnp.where(row8 == 1, cross, 0.0))
        return turned(pair, chosen, HIGH)

    own_row = lax.broadcasted_iota(jnp.int32, (128, 128), 0) // PAR
    own_lane = lax.broadcasted_iota(jnp.int32, (128, 128), 1) // PAR
    lane = lax.broadcasted_iota(jnp.int32, (1, 128), 1)

    def squeeze(block):
        block = jnp.where(own_row == own_lane, block, 0.0)
        return jnp.sum(block.reshape(16, PAR, 128), 0)

    def build(chip, core, sides, diagonal):
        base = base_of(chip, core)
        group = chip * 2 + core
        top = group * 128

        def one(j, index):
            ids = ids_a if index < 2 else ids_b
            slot = ids[index % 2, base + j]
            value = (
                sv[index, 0, pl.ds(slot, 1), :] * full[base + j, 0]
                + sv[index, 1, pl.ds(slot, 1), :] * full[base + j, 1]
                + sv[index, 2, pl.ds(slot, 1), :] * full[base + j, 2]
            )
            times = [
                value * factors[index, k, pl.ds(slot, 1), :]
                for k in range(3)
                if (diagonal if k == 0 else sides)
            ]
            return [value] + times

        def fill(k, second):
            row = pl.multiple_of(top + k * 16, 16)
            inner = pl.multiple_of(k * 16, 16)

            def put(high_ref, low_ref, rows, lanes, value):
                high_ref[pl.ds(rows, 16), lanes], low_ref[pl.ds(rows, 16), lanes] = halves(value)

            gathered = 0.0
            for index in range(4):
                lanes = slice(index * EPOCHS, (index + 1) * EPOCHS)
                a = one(2 * k, index)
                b = one(2 * k + 1, index) if second else [jnp.zeros_like(i) for i in a]
                values = [jnp.concatenate([i, j], axis=0) for i, j in zip(a, b)]
                if diagonal:
                    put(u_high, u_low, inner, lanes, values[1])
                if sides:
                    put(f_high, f_low, row, lanes, values[0])
                    put(t_high, t_low, inner, lanes, values[-2])
                    gathered = gathered + values[-1]
            if sides:
                put(t_high, t_low, inner, slice(4 * EPOCHS, 5 * EPOCHS), gathered)

        def step(k, carry):
            fill(k, True)
            return carry

        lax.fori_loop(0, 7, step, 0)
        fill(7, False)
        if sides:
            side = turned(t_high[...], pick[...]) + turned(t_low[...], pick[...])
            rows = pl.ds(pl.multiple_of(top, 128), 128)
            high, low = halves(side * scale)
            high, low = high.astype(F32), low.astype(F32)
            e_left[rows] = jnp.where(lane < 64, high, low).astype(BF16)
            high, low = halves(side * right_scale)
            high, low = high.astype(F32), low.astype(F32)
            e_right[rows] = jnp.where((lane >= 32) & (lane < 64), low, high).astype(BF16)
        if diagonal:
            rows = pl.ds(pl.multiple_of(top, 128), 128)
            v_high, v_low = f_high[rows], f_low[rows]
            own_sum[chip] = squeeze(
                product(u_high[...], u_low[...], u_high[...], u_low[...])
                - product(v_high, v_low, v_high, v_low)
                - turned(e_left[rows], e_right[rows])
            )

    for copy in keeps[1:]:
        copy.wait()
    hand_a.wait()
    local_rows = prepare(0) + prepare(1)
    for copy in swaps:
        copy.wait_recv()
    hand_b = pltpu.make_async_copy(ids_w, ids_b, local.at[8])
    hand_b.start()
    local_rows = local_rows + prepare(2) + prepare(3)
    scale = jnp.where(lane % 32 < 16, lax.rsqrt(local_rows[0:1] + PRIOR), 0.0)
    right_scale = jnp.where(lane % 32 < 16, scale, 1.0)
    special = jnp.where(lane % 32 == 16, -1.0, local_rows[1:2] * scale)
    hand_b.wait()
    first, second = (share[0], 2), (share[0] + 2, 1)
    share_right.wait_recv()
    far_first = pass_on(left, first, at_y(right))
    twin_left = pass_on(left, share, twin)
    share_left.wait_recv()
    far_second = pass_on(right, second, at_y(left))
    twin_right = pass_on(right, share, twin)
    tail_right = go(own(TAIL), part(y, TAIL), at_y(right))
    head_left = go(own(HEAD), part(y, HEAD), at_y(left))
    build(y, c, True, True)

    head_right.wait_recv()
    far_head = pass_on(left, HEAD, at_y(right))
    mates_left = [pass_on(left, HEAD, mate)]
    tail_left.wait_recv()
    far_tail = pass_on(right, TAIL, at_y(left))
    mates_right = [pass_on(right, TAIL, mate)]
    far_first.wait_recv()
    far_second.wait_recv()
    twin_far = pass_on(far, share, twin)
    mates_far = [pass_on(far, share, mate)]
    twin_left.wait_recv()
    mates_left.append(pass_on(left, REST, mate))
    twin_right.wait_recv()
    mates_right.append(pass_on(right, REST, mate))
    mate_own.wait_recv()
    build(y, 1 - c, True, False)
    tail_right.wait_recv()
    mates_left.append(pass_on(left, TAIL, mate))
    head_left.wait_recv()
    mates_right.append(pass_on(right, HEAD, mate))
    build(left, c, True, True)
    twin_far.wait_recv()
    mates_far.append(pass_on(far, share_twin, mate))
    build(right, c, True, True)
    far_head.wait_recv()
    mates_far.append(pass_on(far, HEAD, mate))
    far_tail.wait_recv()
    mates_far.append(pass_on(far, TAIL, mate))
    for copy in mates_left:
        copy.wait_recv()
    build(left, 1 - c, True, False)
    for copy in mates_right:
        copy.wait_recv()
    build(right, 1 - c, True, False)
    build(far, c, True, False)
    for copy in mates_far:
        copy.wait_recv()
    build(far, 1 - c, True, False)

    row = lax.broadcasted_iota(jnp.int32, (8, 128), 0)
    high, low = halves(jnp.where(row == 0, special, 0.0))
    special = jnp.where(lane < 64, high.astype(F32), low.astype(F32))
    e_left[112:128] = jnp.concatenate(
        [e_left[112:128].astype(F32)[0:8], special], axis=0
    ).astype(BF16)

    def multiply(first, count, slabs):
        rows = slice(first * 128, (first + count) * 128)
        own_rows = [pl.ds(pl.multiple_of((slab * 2 + c) * 128, 128), 128) for slab in slabs]
        r_high, r_low, r_side = [
            jnp.concatenate([ref[i] for i in own_rows], axis=0)
            for ref in (f_high, f_low, e_right)
        ]
        result = product(f_high[rows], f_low[rows], r_high, r_low) + turned(e_left[rows], r_side)
        for i, slab in enumerate(slabs):
            lanes = slice(i * 128, (i + 1) * 128)
            for group in range(count):
                for q in range(NX):
                    at = group * 128 + q * 30
                    normal[slab, first + group, q * COVER : (q + 1) * COVER] = -result[
                        at : at + COVER, lanes
                    ]

    def rows_of(peer):
        return pl.ds(pl.multiple_of(peer * COVER, COVER), COVER)

    row_cut = (pl.ds(0, 64), pl.ds(64, 64))

    def y_first(z0):
        return lambda peer, half: normal.at[peer, pl.ds(z0, 2), row_cut[half]]

    def y_then_x(z0):
        return lambda peer, half: y_part.at[pl.ds(z0 + half, 1), rows_of(peer)]

    def x_first(z0):
        return lambda peer, half: normal.at[pl.ds(2 * half, 2), pl.ds(z0, 2), rows_of(peer)]

    def x_then_y(z0):
        return lambda peer, half: x_part.at[peer, pl.ds(z0 - ZA + half, 1)]

    def small_start(base, source, target, me, size, device):
        copies = []
        for k in range(1, size):
            peer = (me + k) % size
            slot = base + k - 1
            copy = remote(
                source(peer), target.at[me], s_send.at[slot], s_recv.at[slot], device(peer)
            )
            copy.start()
            copies.append(copy)
        return copies

    def small_sum(copies, target, me, own, size):
        target[me] = own
        for copy in copies:
            copy.wait_recv()
        result = target[0]
        for k in range(1, size):
            result = result + target[k]
        return result

    def last_copy(peer, slot):
        return remote(
            total.at[peer], arrived.at[slot], z_send.at[peer], z_recv.at[slot], at_z(peer)
        )

    def send_last(peers):
        for peer in peers:
            @pl.when(z != peer)
            def _():
                last_copy(peer, z).start()

    class Ring:
        def __init__(self, number, view, me, device):
            self.number, self.view, self.me, self.device = number, view, me, device
            self.copies = []

        def start(self, slots=(0, 1, 2, 3)):
            self.copies += ring_start(
                self.view, self.me, bufs[self.number], sems[self.number], self.device, slots
            )

        def middle(self):
            self.copies = ring_middle(
                self.view, self.me, bufs[self.number], sems[self.number], self.device, self.copies
            )

        def finish(self, out_0, out_1):
            ring_finish(self.view, self.me, bufs[self.number], self.copies, out_0, out_1)

    firsts = [
        Ring(0, y_first(0), y, at_y),
        Ring(1, y_first(2), y, at_y),
        Ring(2, x_first(4), x, at_x),
        Ring(3, x_first(6), x, at_x),
    ]
    seconds = [
        Ring(4, y_then_x(0), x, at_x),
        Ring(5, y_then_x(2), x, at_x),
        Ring(6, x_then_y(4), y, at_y),
        Ring(7, x_then_y(6), y, at_y),
    ]

    def turn(k):
        z0 = 2 * k
        if z0 < ZA:
            parts = [y_part.at[pl.ds(z0, 2), row_cut[half]] for half in range(2)]
        else:
            parts = [x_part.at[pl.ds(2 * half, 2), pl.ds(z0 - ZA, 2)] for half in range(2)]
        firsts[k].finish(*parts)
        seconds[k].start()

    def close(k):
        seconds[k].finish(total.at[pl.ds(2 * k, 1)], total.at[pl.ds(2 * k + 1, 1)])
        send_last((2 * k, 2 * k + 1))

    multiply(0, 2, (far, right))
    firsts[0].start((0, 1, 2))
    multiply(4, 2, (far, right))
    multiply(4, 2, (left, y))
    firsts[2].start()
    multiply(0, 2, (left, y))
    firsts[0].start((3,))
    multiply(2, 2, (far, right))
    multiply(2, 2, (left, y))
    multiply(6, 2, (far, right))
    multiply(6, 2, (left, y))
    firsts[0].middle()
    build(far, c, False, True)
    for slab in range(NY):
        small[slab, 0:8] = own_sum[slab]
        small[slab, 8:16] = normal[slab, 0, ROWS : ROWS + 8, :]
    sy = small_start(0, lambda peer: small.at[peer], small_y, y, NY, at_y)

    firsts[1].start()
    firsts[2].middle()
    firsts[3].start()

    turn(0)
    turn(2)
    firsts[1].middle()
    firsts[3].middle()
    hold_x[...] = small_sum(sy, small_y, y, small[y], NY)
    sx = small_start(3, lambda peer: hold_x, small_x, x, NX, at_x)
    seconds[0].middle()
    seconds[2].middle()
    turn(1)
    turn(3)
    close(0)
    close(2)
    hold_z[...] = small_sum(sx, small_x, x, hold_x[...], NX)
    sz = small_start(6, lambda peer: hold_z, small_z, z, NZ, at_z)
    seconds[1].middle()
    seconds[3].middle()
    close(1)
    close(3)

    out_small[...] = small_sum(sz, small_z, z, hold_z[...], NZ)
    value = total[z]
    for k in (1, 7, 2, 6, 3, 5, 4):
        peer = (z + k) % NZ
        last_copy(peer, peer).wait_recv()
        value = value + arrived[peer]
    out[...] = value
    for copies in [everything, sy, sx, sz] + [ring.copies for ring in firsts + seconds]:
        for copy in copies:
            copy.wait_send()
    for k in range(1, NZ):
        last_copy((z + k) % NZ, z).wait_send()


def finish_kernel(block, sums, owned, right, blocks):
    z, x, y, c = place()
    cross_factor = SATS / math.sqrt(512 * EPOCHS)
    factor = SATS / (512 * SLOTS * EPOCHS)
    value = block[0:30, 0:ROWS]
    row = (z * NX + x) * 30 + lax.broadcasted_iota(jnp.int32, (30, ROWS), 0)
    column = (y * 2 + c) * ROWS + lax.broadcasted_iota(jnp.int32, (30, ROWS), 1)
    owned[...] = jnp.where(row // PAR == column // PAR, 0.0, value) * cross_factor
    right[...] = sums[14:15, 0:ROWS] * factor
    scaled = jnp.broadcast_to((sums[0:8] * factor)[:, None, :], (PAR, PAR, 128))
    place_of = lax.broadcasted_iota(jnp.int32, (PAR, PAR, 128), 2) % PAR
    inner = lax.broadcasted_iota(jnp.int32, (PAR, PAR, 128), 1)
    rows = jnp.where(place_of == inner, scaled, 0.0).reshape(PAR * PAR, 128)
    to = lax.broadcasted_iota(jnp.int32, (128, 128), 0)
    lane = lax.broadcasted_iota(jnp.int32, (128, 128), 1)
    moved = turned(rows, jnp.where(to == lane // PAR, 1.0, 0.0), HIGH)
    blocks[...] = moved.reshape(PAR, PAR, 128)[:, :, 0:OWN]


def ring_buffers(half_0, half_1):
    shapes = [half_0, half_1, half_0, half_1, half_0, half_1, half_0, half_1]
    return [pltpu.VMEM(shape, F32) for shape in shapes]


def shards(sight, mapping, residual, counts, track, knots, orbit):
    shape = jax.ShapeDtypeStruct
    stations = (sight, mapping, residual, counts, knots)
    nb = NZ - ZA
    big = 4 * EPOCHS
    scratch = (
        [pltpu.VMEM(a.shape, a.dtype) for a in stations] * 2
        + [
            pltpu.SMEM((2, SLOTS), jnp.int32),
            pltpu.VMEM((2, 128), jnp.int32),
            pltpu.VMEM((2, 128), jnp.int32),
            pltpu.SMEM((2, 128), jnp.int32),
            pltpu.SMEM((2, 128), jnp.int32),
            pltpu.VMEM((SATS, 3, PAR, EPOCHS), F32),
            pltpu.VMEM((4, 3, SLOTS + 8, EPOCHS), F32),
            pltpu.VMEM((4, 3, SLOTS + 8, EPOCHS), F32),
            pltpu.VMEM((1024, big), BF16),
            pltpu.VMEM((1024, big), BF16),
            pltpu.VMEM((128, big), BF16),
            pltpu.VMEM((128, big), BF16),
            pltpu.VMEM((128, big + EPOCHS), BF16),
            pltpu.VMEM((128, big + EPOCHS), BF16),
            pltpu.VMEM((128, big + EPOCHS), BF16),
            pltpu.VMEM((1024, 128), BF16),
            pltpu.VMEM((1024, 128), BF16),
            pltpu.VMEM((NY, NZ, 128, 128), F32),
            pltpu.VMEM((NY, PAR, 128), F32),
            pltpu.VMEM((NY, 16, 128), F32),
        ]
        + ring_buffers((2, 64, 128), (2, 64, 128)) * 2
        + ring_buffers((2, 2, COVER, 128), (2, 2, COVER, 128)) * 2
        + ring_buffers((1, COVER, 128), (1, COVER, 128)) * 4
        + [
            pltpu.VMEM((ZA, 128, 128), F32),
            pltpu.VMEM((NY, nb, COVER, 128), F32),
            pltpu.VMEM((NZ, COVER, 128), F32),
            pltpu.VMEM((NZ, COVER, 128), F32),
            pltpu.VMEM((NY, 16, 128), F32),
            pltpu.VMEM((NX, 16, 128), F32),
            pltpu.VMEM((NZ, 16, 128), F32),
            pltpu.VMEM((16, 128), F32),
            pltpu.VMEM((16, 128), F32),
            pltpu.SemaphoreType.DMA((30,)),
            pltpu.SemaphoreType.DMA((30,)),
            pltpu.SemaphoreType.DMA((9,)),
        ]
        + [pltpu.SemaphoreType.DMA((6,))] * 16
        + [
            pltpu.SemaphoreType.DMA((NZ,)),
            pltpu.SemaphoreType.DMA((NZ,)),
            pltpu.SemaphoreType.DMA((13,)),
            pltpu.SemaphoreType.DMA((13,)),
        ]
    )
    block, sums = pl.pallas_call(
        main_kernel,
        name="network",
        out_shape=[shape((COVER, 128), F32), shape((16, 128), F32)],
        in_specs=[ANY] * 7,
        out_specs=[VMEM, VMEM],
        scratch_shapes=scratch,
        compiler_params=pltpu.CompilerParams(
            collective_id=0, has_side_effects=True, vmem_limit_bytes=60 * 1024 * 1024
        ),
    )(track, orbit, *stations)

    owned, right, blocks = pl.pallas_call(
        finish_kernel,
        name="finish",
        out_shape=[
            shape((30, ROWS), F32),
            shape((1, ROWS), F32),
            shape((PAR, PAR, OWN), F32),
        ],
        in_specs=[VMEM, VMEM],
        out_specs=[VMEM] * 3,
    )(block, sums)
    return owned.T, right.reshape(ROWS), jnp.transpose(blocks, (2, 0, 1))


def solution(mesh):
    placed = (
        P(("sta", "sat"), None, None, None),
        P(("sta", "sat"), None, None),
        P(("sta", "sat"), None, None),
        P(("sta", "sat"), None, None),
        P(("sta", "sat"), None),
        P(("sta", "sat"), None),
        P("sat", None, None, None),
    )
    return jax.shard_map(
        shards,
        mesh=mesh,
        in_specs=placed,
        out_specs=(P("sat", "sta"), P("sat"), P("sat", None, None)),
        check_vma=False,
    )
```
